32 devices in a mesh: group: 2 (over y), chan: 4 (over x, core), tm: 4 (over z).
Axes of the slice: x: 2, y: 2, z: 4, core: 2. Of those that a mesh axis runs over, the one named last changes fastest.
Arguments:
- voltages: bfloat16 [2, 32, 1024, 1024], P(None, ('group', 'tm'), 'chan'), parts along dimension 1, may hold values from -6 to 6
- feed_position: int32 [1024, 2], replicated, may hold values from 0 to 63
- beam_steering: int32 [256, 2], P('group'), parts along dimension 0, may hold values from 0 to 63
- synthesis_taps: float32 [4, 1024], replicated, may hold values from 0.2 to 1
Outputs:
- synthesized: bfloat16 [2, 128, 32, 1024], P(None, 'chan', ('group', 'tm')), parts along dimension 2
The draws below stay inside these ranges and needn't reach their ends.
There are 2 independent parts, one for each index of `group`. The reference program is written for one: setup_inputs(seed, part) draws one part's arguments, and reference() takes and returns one part's arrays. A program takes and returns all parts, laid end to end along the dimension named above; an argument that names none is the same for every part. Nothing has to cross between parts.
All inputs are finite; a program needn't handle non-finite values.
Results may differ from the reference program's by a relative error of at most 0.0085.
Values may be sent and summed in bfloat16 or wider, within the bound.
No kernel may reach another device: no remote copies, remote signals or barrier semaphores. Data moves between devices by JAX's collectives and lax.ppermute only.
A program may use at most 64 MiB of HBM per device.

```python
import math
import jax
import jax.numpy as jnp
from jax import lax

F = 1024
C = 1024
BEAMS = 128
TAPS = 4
PHASES = 4096
FRAMES = 16


def touch_ends(drawn, stream_key, smallest, top_value):
    spot = [jax.random.randint(jax.random.fold_in(stream_key, axis), (), 0, length) for axis, length in enumerate(drawn.shape)]
    main_axis = drawn.shape.index(max(drawn.shape))
    beside = spot[:main_axis] + [(spot[main_axis] + 1) % drawn.shape[main_axis]] + spot[main_axis + 1:]
    return drawn.at[tuple(spot)].set(smallest).at[tuple(beside)].set(top_value)


def block_levels(rng, shape, cuts, least, top_value):
    level, own = 1.0, jax.random.fold_in(rng, 6)
    for axis_at, blocks in cuts:
        draws = jnp.exp(jax.random.uniform(jax.random.fold_in(own, axis_at), (blocks,), jnp.float32, least / len(cuts), top_value / len(cuts)))
        level = level * jnp.repeat(draws, shape[axis_at] // blocks).reshape([-1 if axis == axis_at else 1 for axis in range(len(shape))])
    return level


def gaussian(rng, dims, deviation, most, cuts=(), kind=jnp.bfloat16):
    entries = deviation * jax.random.normal(rng, dims, jnp.float32)
    if cuts:
        entries = entries * block_levels(rng, dims, cuts, -0.22, 0.18)
    return jnp.clip(entries, -most, most).astype(kind)


def setup_inputs(seed: int = 0, part: int = 0) -> dict:
    key_of = jax.random.split(jax.random.key(seed), 5)
    part_splits = jax.random.split(jax.random.fold_in(key_of[4], part), 5)
    return {
        "voltages": gaussian(part_splits[0], (2, FRAMES, F, C), 1.0, 6.0, ((1, 4), (2, 4))),
        "feed_position": touch_ends(jax.random.randint(key_of[1], (F, 2), 0, 64), jax.random.fold_in(key_of[1], 1), 0, 63).astype(jnp.int32),
        "beam_steering": touch_ends(jax.random.randint(part_splits[2], (BEAMS, 2), 0, 64), jax.random.fold_in(part_splits[2], 1), 0, 63).astype(jnp.int32),
        "synthesis_taps": jnp.clip(jax.random.uniform(key_of[3], (TAPS, C), jnp.float32, 0.2, 1.0), 0.2, 1.0),
    }


def compute_delays(feed_position, beam_steering):
    first = feed_position[:, 0:1] * beam_steering[:, 0][None, :]
    second = feed_position[:, 1:2] * beam_steering[:, 1][None, :]
    return (first + second) % PHASES

def make_weights(delays, channel_ids):
    phases = channel_ids[:, None, None] * delays[None, :, :] % PHASES
    angles = phases.astype(jnp.float32) * (2.0 * math.pi / PHASES)
    return jnp.concatenate([jnp.cos(angles), jnp.sin(angles)], axis=-1).astype(jnp.bfloat16)

def combine(product):
    half = product.shape[-1] // 2
    real_part = product[0, ..., :half] - product[1, ..., half:]
    imag_part = product[0, ..., half:] + product[1, ..., :half]
    return (jnp.stack([real_part, imag_part]) * (1.0 / math.sqrt(F))).astype(jnp.bfloat16)

def make_basis():
    rows = jnp.arange(C, dtype=jnp.int32)
    products = rows[:, None] * rows[None, :] % C
    angles = products.astype(jnp.float32) * (2.0 * math.pi / C)
    cosine = jnp.cos(angles)
    sine = jnp.sin(angles)
    upper = jnp.concatenate([cosine, sine], axis=1)
    lower = jnp.concatenate([-sine, cosine], axis=1)
    return jnp.stack([upper, lower]).astype(jnp.bfloat16)

def reference(voltages, feed_position, beam_steering, synthesis_taps):
    delays = compute_delays(feed_position, beam_steering)
    frame_count = voltages.shape[1]
    width = math.gcd(C, 8)
    count = C // width

    def one_block(block_index):
        offset = block_index * width
        slab = lax.dynamic_slice_in_dim(voltages, offset, width, 3)
        channel_ids = offset + jnp.arange(width, dtype=jnp.int32)
        weights = make_weights(delays, channel_ids)
        product = jnp.einsum('stfc,cfk->stck', slab.astype(jnp.float32), weights.astype(jnp.float32))
        return combine(product)
    blocks = lax.map(one_block, jnp.arange(count, dtype=jnp.int32))
    beamed = jnp.transpose(blocks, (1, 2, 0, 3, 4)).reshape(2, frame_count, C, BEAMS)
    basis = make_basis()
    frames = jnp.einsum('stcb,scn->tbn', beamed.astype(jnp.float32), basis.astype(jnp.float32))
    frames = (frames * (1.0 / math.sqrt(C))).astype(jnp.bfloat16)
    leading = jnp.zeros((TAPS - 1,) + frames.shape[1:], jnp.bfloat16)
    extended = jnp.concatenate([leading, frames], axis=0).astype(jnp.float32)
    doubled = jnp.concatenate([synthesis_taps, synthesis_taps], axis=1)
    total = jnp.zeros(frames.shape, jnp.float32)
    for tap_index in range(TAPS):
        begin = TAPS - 1 - tap_index
        total = total + doubled[tap_index][None, None, :] * extended[begin:begin + frame_count]
    output = total.astype(jnp.bfloat16).reshape(frame_count, BEAMS, 2, C)
    return jnp.transpose(output, (2, 1, 0, 3))
```

```python
import math

import jax
import jax.numpy as jnp
from jax import lax
from jax.experimental import pallas as pl
from jax.experimental.pallas import tpu as pltpu
from jax.sharding import PartitionSpec as P

PHASES = 4096
LANES = 128
HALF = 32


def turn(phase, steps):
    quarter = steps // 4
    quadrant = (phase + quarter // 2) // quarter
    rest = (phase - quadrant * quarter).astype(jnp.float32) * (2.0 * math.pi / steps)
    square = rest * rest
    sine = rest * (1.0 + square * (-1.6666666e-1 + square * (8.3333310e-3 + square * (-1.9840874e-4 + square * 2.7525562e-6))))
    cosine = 1.0 + square * (-0.5 + square * (4.1666666e-2 + square * (-1.3888889e-3 + square * (2.4801587e-5 - square * 2.7557319e-7))))
    odd = (quadrant & 1) == 1
    real = jnp.where(odd, sine, cosine)
    imag = jnp.where(odd, cosine, sine)
    real = jnp.where(((quadrant + 1) & 2) == 2, -real, real)
    imag = jnp.where((quadrant & 2) == 2, -imag, imag)
    return real, imag


def times(a, b):
    return a[0] * b[0] - a[1] * b[1], a[0] * b[1] + a[1] * b[0]


def beam_kernel(position, steering, voltages, keep, send, delays, centre_tables, offset_tables, rows, turned_rows, sums):
    feeds, beams = delays.shape
    frames = voltages.shape[1]
    stride = 2 * frames
    block = voltages.shape[3]
    devices = 2 * keep.shape[0]
    own_beams = beams // devices
    centres = centre_tables.shape[1]
    step = pl.program_id(0)
    here = lax.axis_index("chan")

    @pl.when(step == 0)
    def _():
        def column(axis):
            first = here * feeds if position.shape[1] > feeds else 0
            row = position[axis : axis + 1, pl.ds(pl.multiple_of(first, LANES), feeds)].astype(jnp.float32)
            return jnp.transpose(jnp.broadcast_to(row, (beams, feeds))).astype(jnp.int32)

        total = column(0) * steering[0:1, :] + column(1) * steering[1:2, :]
        delays[...] = total & (PHASES - 1)

        def one_slab(index, carry):
            at = pl.multiple_of(index * 16, 16)
            delay = delays[pl.ds(at, 16), :]
            half_step = turn(delay, 2 * PHASES)
            state = half_step
            advance = times(half_step, half_step)
            for offset in range(HALF):
                offset_tables[0, offset, pl.ds(at, 16), :] = state[0].astype(jnp.bfloat16)
                offset_tables[1, offset, pl.ds(at, 16), :] = state[1].astype(jnp.bfloat16)
                if offset + 1 < HALF:
                    state = times(state, advance)
            state = turn(((2 * HALF - 1) * delay) & (2 * PHASES - 1), 2 * PHASES)
            advance = turn((4 * HALF * delay) & (2 * PHASES - 1), 2 * PHASES)
            for centre in range(centres):
                centre_tables[0, centre, pl.ds(at, 16), :] = state[0].astype(jnp.bfloat16)
                centre_tables[1, centre, pl.ds(at, 16), :] = state[1].astype(jnp.bfloat16)
                centre_tables[2, centre, pl.ds(at, 16), :] = (-state[1]).astype(jnp.bfloat16)
                if centre + 1 < centres:
                    state = times(state, advance)
            return carry

        lax.fori_loop(0, feeds // 16, one_slab, 0)

    width = min(feeds, LANES)
    for part in range(2):
        for frame in range(frames):
            slot = part * frames + frame
            other = (1 - part) * frames + frame
            for at in range(feeds // width):
                piece = voltages[part, frame, at * width : (at + 1) * width, :].astype(jnp.float32)
                if width < LANES:
                    piece = jnp.concatenate([piece, jnp.zeros((LANES - width, block), jnp.float32)], axis=0)
                piece = jnp.transpose(piece)
                rows[at, pl.ds(slot, block, stride=stride), :] = piece
                turned_rows[at, pl.ds(other, block, stride=stride), :] = piece if part == 0 else -piece

    def lhs(scratch, upper, lower):
        pieces = []
        for at in range(feeds // width):
            top = scratch[at, pl.ds(pl.multiple_of(upper * stride, stride), stride), :]
            bottom = scratch[at, pl.ds(pl.multiple_of(lower * stride, stride), stride), :]
            pieces.append(jnp.concatenate([top, bottom], axis=0))
        return jnp.concatenate(pieces, axis=1).astype(jnp.bfloat16)[:, :feeds]

    def one_pair(index, carry):
        local = index // HALF
        offset = index % HALF
        centre = step * (block // (2 * HALF)) + local
        upper = local * 2 * HALF + HALF + offset
        lower = local * 2 * HALF + HALF - 1 - offset
        cosine = centre_tables[0, centre]
        sine = centre_tables[1, centre]
        minus = centre_tables[2, centre]
        small_cosine = offset_tables[0, offset]
        small_sine = offset_tables[1, offset]
        first = jnp.concatenate([cosine * small_cosine, minus * small_sine], axis=1)
        second = jnp.concatenate([sine * small_cosine, cosine * small_sine], axis=1)
        total = jnp.dot(lhs(rows, upper, lower), first, preferred_element_type=jnp.float32)
        total = total + jnp.dot(lhs(turned_rows, upper, lower), second, preferred_element_type=jnp.float32)
        sums[pl.ds(pl.multiple_of(upper * stride, stride), stride), :] = total[:stride, :beams] + total[:stride, beams:]
        sums[pl.ds(pl.multiple_of(lower * stride, stride), stride), :] = total[stride:, :beams] - total[stride:, beams:]
        return carry

    lax.fori_loop(0, block // 2, one_pair, 0, unroll=2)

    scale = 1.0 / math.sqrt(feeds * devices)
    for part in range(2):
        for frame in range(frames):
            slot = part * frames + frame
            piece = jnp.transpose(sums[pl.ds(slot, block, stride=stride), :] * scale)
            for target in range(devices):
                value = piece[target * own_beams : (target + 1) * own_beams, :].astype(jnp.bfloat16)
                relative = target ^ here

                @pl.when(relative % 2 == 0)
                def _():
                    keep[relative // 2, frame, part] = value

                @pl.when(relative % 2 == 1)
                def _():
                    send[relative // 2, frame, part] = value


def beamform(voltages, position, steering, devices):
    _, frames, feeds, channels = voltages.shape
    beams = steering.shape[1]
    block = LANES
    width = min(feeds, LANES)
    shape = jax.ShapeDtypeStruct((devices // 2, frames, 2, beams // devices, channels), jnp.bfloat16)
    spec = pl.BlockSpec((devices // 2, frames, 2, beams // devices, block), lambda i: (0, 0, 0, 0, i))
    return pl.pallas_call(
        beam_kernel,
        grid=(channels // block,),
        in_specs=[
            pl.BlockSpec(position.shape, lambda i: (0, 0)),
            pl.BlockSpec(steering.shape, lambda i: (0, 0)),
            pl.BlockSpec((2, frames, feeds, block), lambda i: (0, 0, 0, i)),
        ],
        out_specs=[spec, spec],
        out_shape=[shape, shape],
        scratch_shapes=[
            pltpu.VMEM((feeds, beams), jnp.int32),
            pltpu.VMEM((3, channels // (2 * HALF), feeds, beams), jnp.bfloat16),
            pltpu.VMEM((2, HALF, feeds, beams), jnp.bfloat16),
            pltpu.VMEM((feeds // width, block * 2 * frames, LANES), jnp.float32),
            pltpu.VMEM((feeds // width, block * 2 * frames, LANES), jnp.float32),
            pltpu.VMEM((block * 2 * frames, beams), jnp.float32),
        ],
        compiler_params=pltpu.CompilerParams(vmem_limit_bytes=48 * 2**20),
        name="beam",
    )(position, steering, voltages)


def synth_kernel(own, halo, taps, out, basis_real, basis_imag, small):
    frames, _, beams, channels = own.shape
    before = halo.shape[0]
    width = out.shape[3]
    first = pl.program_id(0) * width
    group = small.shape[1]

    def phases(rows, factor):
        row = lax.broadcasted_iota(jnp.int32, (rows, width), 0) * factor
        column = first + lax.broadcasted_iota(jnp.int32, (rows, width), 1)
        return (row * column) & (channels - 1)

    real, imag = turn(phases(group, 1), channels)
    small[0] = real
    small[1] = imag
    count = channels // group
    large = turn(phases(count, group), channels)
    for index in range(count):
        a = (large[0][index : index + 1], large[1][index : index + 1])
        value = times(a, (small[0], small[1]))
        basis_real[index * group : (index + 1) * group, :] = value[0].astype(jnp.bfloat16)
        basis_imag[index * group : (index + 1) * group, :] = value[1].astype(jnp.bfloat16)

    def gather(part):
        pieces = [halo[t, part] for t in range(before)] + [own[t, part] for t in range(frames)]
        return jnp.concatenate(pieces, axis=0)

    beams_real = gather(0)
    beams_imag = gather(1)

    def dot(a, b):
        return jnp.dot(a, b[...], preferred_element_type=jnp.float32)

    scale = 1.0 / math.sqrt(channels)
    total_real = (dot(beams_real, basis_real) - dot(beams_imag, basis_imag)) * scale
    total_imag = (dot(beams_real, basis_imag) + dot(beams_imag, basis_real)) * scale
    count_taps = taps.shape[0]
    for part, total in enumerate((total_real, total_imag)):
        rounded = total.astype(jnp.bfloat16).astype(jnp.float32)
        for t in range(frames):
            value = jnp.zeros((beams, width), jnp.float32)
            for k in range(count_taps):
                at = before + t - k
                value = value + taps[k : k + 1, :] * rounded[at * beams : (at + 1) * beams]
            out[part, t] = value.astype(jnp.bfloat16)


def synthesize(own, halo, taps):
    frames, _, beams, channels = own.shape
    width = min(256, channels)
    return pl.pallas_call(
        synth_kernel,
        grid=(channels // width,),
        in_specs=[
            pl.BlockSpec(own.shape, lambda i: (0, 0, 0, 0)),
            pl.BlockSpec(halo.shape, lambda i: (0, 0, 0, 0)),
            pl.BlockSpec((taps.shape[0], width), lambda i: (0, i)),
        ],
        out_specs=pl.BlockSpec((2, frames, beams, width), lambda i: (0, 0, 0, i)),
        out_shape=jax.ShapeDtypeStruct((2, frames, beams, channels), jnp.bfloat16),
        scratch_shapes=[
            pltpu.VMEM((channels, width), jnp.bfloat16),
            pltpu.VMEM((channels, width), jnp.bfloat16),
            pltpu.VMEM((2, 32, width), jnp.float32),
        ],
        compiler_params=pltpu.CompilerParams(vmem_limit_bytes=48 * 2**20),
        name="synth",
    )(own, halo, taps)


def added(*terms):
    return sum(term.astype(jnp.float32) for term in terms).astype(jnp.bfloat16)


def on_device(voltages, feed_position, beam_steering, synthesis_taps):
    devices = lax.axis_size("chan")
    steps = lax.axis_size("tm")
    taps = synthesis_taps.shape[0]
    feeds = voltages.shape[2]
    position = feed_position.T
    if feeds % LANES:
        position = lax.dynamic_slice_in_dim(position, lax.axis_index("chan") * feeds, feeds, 1)
    keep, send = beamform(voltages, position, beam_steering.T, devices)
    mask = 1
    while True:
        arrived = lax.ppermute(send, "chan", [(i, i ^ mask) for i in range(devices)])
        mask *= 2
        if mask == devices:
            break
        send = added(keep[1::2], arrived[1::2])
        keep = added(keep[0::2], arrived[0::2])
    own = added(keep[0], arrived[0])
    halo = lax.ppermute(own[own.shape[0] - (taps - 1) :], "tm", [(i, i + 1) for i in range(steps - 1)])
    out = synthesize(own, halo, synthesis_taps)
    return jnp.transpose(out, (0, 2, 1, 3))


def solution(mesh):
    return jax.shard_map(
        on_device,
        mesh=mesh,
        in_specs=(P(None, ("group", "tm"), "chan", None), P(), P("group", None), P()),
        out_specs=P(None, "chan", ("group", "tm"), None),
        check_vma=False,
    )
```

```python
import functools
import math

import jax
import jax.numpy as jnp
from jax import lax
from jax.experimental import pallas as pl
from jax.experimental.pallas import tpu as pltpu
from jax.sharding import PartitionSpec as P

PHASES = 4096
LANES = 128
HALF = 32
SLAB = 16
TABLE = jnp.float32


def turn(phase, steps):
    quarter = steps // 4
    shift = quarter.bit_length() - 1
    quadrant = lax.shift_right_logical(phase + quarter // 2, shift)
    rest = (phase - lax.shift_left(quadrant, shift)).astype(jnp.float32) * (2.0 * math.pi / steps)
    square = rest * rest
    sine = rest * (1.0 + square * (-1.6666666e-1 + square * (8.3333310e-3 + square * (-1.9840874e-4 + square * 2.7525562e-6))))
    cosine = 1.0 + square * (-0.5 + square * (4.1666666e-2 + square * (-1.3888889e-3 + square * (2.4801587e-5 - square * 2.7557319e-7))))
    odd = (quadrant & 1) == 1
    real = jnp.where(odd, sine, cosine)
    imag = jnp.where(odd, cosine, sine)
    real = jnp.where(((quadrant + 1) & 2) == 2, -real, real)
    imag = jnp.where((quadrant & 2) == 2, -imag, imag)
    return real, imag


def times(a, b):
    return a[0] * b[0] - a[1] * b[1], a[0] * b[1] + a[1] * b[0]


def beam_kernel(first, position, steering, voltages, keep, send, staged, arrivals, centre_tables, offset_tables, rows_even, rows_odd, sums_even, sums_odd):
    feeds, beams = offset_tables.shape[2:]
    frames = voltages.shape[1]
    stride = 2 * frames
    block = rows_even.shape[1] // stride
    devices = 2 * keep.shape[0]
    own_beams = beams // devices
    centres = centre_tables.shape[1]
    blocks = staged.shape[0]
    here = lax.axis_index("chan")
    rows_of = (rows_even, rows_odd)
    sums_of = (sums_even, sums_odd)

    def arrival(index):
        source = voltages.at[:, :, :, pl.ds(first + index * block, block)]
        return pltpu.make_async_copy(source, staged.at[index], arrivals.at[index])

    for index in range(blocks):
        arrival(index).start()

    def column(axis):
        start = here * feeds if position.shape[1] > feeds else 0
        row = position[axis : axis + 1, pl.ds(pl.multiple_of(start, LANES), feeds)].astype(jnp.float32)
        return jnp.transpose(jnp.broadcast_to(row, (beams, feeds))).astype(jnp.int32)

    lane = lax.broadcasted_iota(jnp.int32, steering.shape, 1)
    aim = steering[...]
    size = own_beams
    while size < beams:
        upper = (lane & size) != 0
        swapped = jnp.where(upper, pltpu.roll(aim, size, 1), pltpu.roll(aim, beams - size, 1))
        aim = jnp.where((here & (size // own_beams)) != 0, swapped, aim)
        size *= 2
    total = column(0) * aim[0:1, :] + column(1) * aim[1:2, :]
    offset_tables[0, 0] = (total & (PHASES - 1)).astype(TABLE)

    def one_slab(index, carry):
        at = pl.multiple_of(index * SLAB, SLAB)
        delay = offset_tables[0, 0, pl.ds(at, SLAB), :].astype(jnp.int32)
        half_step = turn(delay, 2 * PHASES)
        state = half_step
        advance = times(half_step, half_step)
        for offset in range(HALF):
            offset_tables[0, offset, pl.ds(at, SLAB), :] = state[0].astype(TABLE)
            offset_tables[1, offset, pl.ds(at, SLAB), :] = state[1].astype(TABLE)
            if offset + 1 < HALF:
                state = times(state, advance)
        state = turn(((2 * first + 2 * HALF - 1) * delay) & (2 * PHASES - 1), 2 * PHASES)
        advance = turn((4 * HALF * delay) & (2 * PHASES - 1), 2 * PHASES)
        for centre in range(centres):
            centre_tables[0, centre, pl.ds(at, SLAB), :] = state[0].astype(TABLE)
            centre_tables[1, centre, pl.ds(at, SLAB), :] = state[1].astype(TABLE)
            if centre + 1 < centres:
                state = times(state, advance)
        return carry

    lax.fori_loop(0, feeds // SLAB, one_slab, 0)
    for index in range(blocks):
        arrival(index).wait()

    width = min(feeds, LANES)
    scale = 1.0 / math.sqrt(feeds * devices)
    sign = jnp.where(lax.broadcasted_iota(jnp.int32, (stride, beams), 0) < frames, -1.0, 1.0)

    def take(index, rows, slot):
        for at in range(feeds // width):
            piece = staged[index, slot // frames, slot % frames, at * width : (at + 1) * width, :].astype(jnp.float32)
            if width < LANES:
                piece = jnp.concatenate([piece, jnp.zeros((LANES - width, block), jnp.float32)], axis=0)
            rows[at, pl.ds(slot, block, stride=stride), :] = jnp.transpose(piece)

    def give(index, sums, slot):
        piece = jnp.transpose(sums[pl.ds(slot, block, stride=stride), :] * scale)
        for relative in range(devices):
            value = piece[relative * own_beams : (relative + 1) * own_beams, :].astype(jnp.bfloat16)
            out = send if relative % 2 else keep
            out[relative // 2, slot % frames, slot // frames, :, pl.ds(pl.multiple_of(index * block, block), block)] = value

    def quarter_turn(value):
        return pltpu.roll(value, frames, 0) * sign

    def dot(a, b):
        return jnp.dot(a, b, preferred_element_type=jnp.float32)

    def pair(rows, sums, cosine, sine, local, offset):
        upper = local * 2 * HALF + HALF + offset
        lower = local * 2 * HALF + HALF - 1 - offset
        pieces = []
        for at in range(feeds // width):
            top = rows[at, upper * stride : (upper + 1) * stride, :]
            bottom = rows[at, lower * stride : (lower + 1) * stride, :]
            pieces.append(jnp.concatenate([top, bottom], axis=0))
        left = jnp.concatenate(pieces, axis=1).astype(jnp.bfloat16)[:, :feeds]
        small_cosine = offset_tables[0, offset].astype(jnp.bfloat16)
        small_sine = offset_tables[1, offset].astype(jnp.bfloat16)
        straight = dot(left, jnp.concatenate([cosine * small_cosine, sine * small_sine], axis=1))
        crossed = dot(left, jnp.concatenate([sine * small_cosine, cosine * small_sine], axis=1))
        a, b, c, d = straight[:, :beams], straight[:, beams:], crossed[:, :beams], crossed[:, beams:]
        more = quarter_turn(c[:stride] + d[:stride])
        less = quarter_turn(c[stride:] - d[stride:])
        sums[upper * stride : (upper + 1) * stride, :] = a[:stride] - b[:stride] + more
        sums[lower * stride : (lower + 1) * stride, :] = a[stride:] + b[stride:] + less

    def one_block(index, parity):
        rows, sums = rows_of[parity], sums_of[parity]
        every = HALF * (block // (2 * HALF)) // stride
        for local in range(block // (2 * HALF)):
            centre = index * (block // (2 * HALF)) + local
            cosine = centre_tables[0, centre].astype(jnp.bfloat16)
            sine = centre_tables[1, centre].astype(jnp.bfloat16)
            for offset in range(HALF):
                count = local * HALF + offset
                if count % every == 0:
                    give(jnp.maximum(index - 1, 0), sums_of[1 - parity], count // every)
                    take(jnp.minimum(index + 1, blocks - 1), rows_of[1 - parity], count // every)
                pair(rows, sums, cosine, sine, local, offset)

    for slot in range(stride):
        take(0, rows_even, slot)

    def two_blocks(index, carry):
        one_block(2 * index, 0)
        one_block(2 * index + 1, 1)
        return carry

    lax.fori_loop(0, blocks // 2, two_blocks, 0)
    for slot in range(stride):
        give(blocks - 1, sums_odd, slot)


def beamform(voltages, position, steering, devices, first, count):
    _, frames, feeds, _ = voltages.shape
    beams = steering.shape[1]
    width = min(feeds, LANES)
    shape = jax.ShapeDtypeStruct((devices // 2, frames, 2, beams // devices, count), jnp.bfloat16)
    rows = pltpu.VMEM((feeds // width, LANES * 2 * frames, LANES), jnp.float32)
    sums = pltpu.VMEM((LANES * 2 * frames, beams), jnp.float32)
    work = 2 * frames * 2 * feeds * beams * count
    whole = pl.BlockSpec(memory_space=pltpu.VMEM)
    return pl.pallas_call(
        functools.partial(beam_kernel, first),
        in_specs=[whole, whole, pl.BlockSpec(memory_space=pl.ANY)],
        out_specs=[whole, whole],
        out_shape=[shape, shape],
        scratch_shapes=[
            pltpu.VMEM((count // LANES, 2, frames, feeds, LANES), jnp.bfloat16),
            pltpu.SemaphoreType.DMA((count // LANES,)),
            pltpu.VMEM((2, count // (2 * HALF), feeds, beams), TABLE),
            pltpu.VMEM((2, HALF, feeds, beams), TABLE),
            rows,
            rows,
            sums,
            sums,
        ],
        compiler_params=pltpu.CompilerParams(vmem_limit_bytes=48 * 2**20),
        cost_estimate=pl.CostEstimate(flops=32 * work, bytes_accessed=4 * 2 * frames * feeds * count, transcendentals=0),
        name="beam",
    )(position, steering, voltages)


def synth_kernel(own, halo, taps, out, basis_real, basis_imag, small):
    frames, _, beams, channels = own.shape
    before = halo.shape[0]
    width = out.shape[3]
    first = pl.program_id(0) * width
    group = small.shape[1]

    def phases(rows, factor):
        row = lax.broadcasted_iota(jnp.int32, (rows, width), 0) * factor
        column = first + lax.broadcasted_iota(jnp.int32, (rows, width), 1)
        return (row * column) & (channels - 1)

    real, imag = turn(phases(group, 1), channels)
    small[0] = real
    small[1] = imag
    count = channels // group
    large = turn(phases(count, group), channels)
    for index in range(count):
        a = (large[0][index : index + 1], large[1][index : index + 1])
        value = times(a, (small[0], small[1]))
        basis_real[index * group : (index + 1) * group, :] = value[0].astype(jnp.bfloat16)
        basis_imag[index * group : (index + 1) * group, :] = value[1].astype(jnp.bfloat16)

    def gather(part):
        pieces = [halo[t, part] for t in range(before)] + [own[t, part] for t in range(frames)]
        return jnp.concatenate(pieces, axis=0)

    beams_real = gather(0)
    beams_imag = gather(1)

    def dot(a, b):
        return jnp.dot(a, b[...], preferred_element_type=jnp.float32)

    scale = 1.0 / math.sqrt(channels)
    total_real = (dot(beams_real, basis_real) - dot(beams_imag, basis_imag)) * scale
    total_imag = (dot(beams_real, basis_imag) + dot(beams_imag, basis_real)) * scale
    count_taps = taps.shape[0]
    for part, total in enumerate((total_real, total_imag)):
        rounded = total.astype(jnp.bfloat16).astype(jnp.float32)
        for t in range(frames):
            value = jnp.zeros((beams, width), jnp.float32)
            for k in range(count_taps):
                at = before + t - k
                value = value + taps[k : k + 1, :] * rounded[at * beams : (at + 1) * beams]
            out[part, t] = value.astype(jnp.bfloat16)


def synthesize(own, halo, taps):
    frames, _, beams, channels = own.shape
    width = min(256, channels)
    return pl.pallas_call(
        synth_kernel,
        grid=(channels // width,),
        in_specs=[
            pl.BlockSpec(own.shape, lambda i: (0, 0, 0, 0)),
            pl.BlockSpec(halo.shape, lambda i: (0, 0, 0, 0)),
            pl.BlockSpec((taps.shape[0], width), lambda i: (0, i)),
        ],
        out_specs=pl.BlockSpec((2, frames, beams, width), lambda i: (0, 0, 0, i)),
        out_shape=jax.ShapeDtypeStruct((2, frames, beams, channels), jnp.bfloat16),
        scratch_shapes=[
            pltpu.VMEM((channels, width), jnp.bfloat16),
            pltpu.VMEM((channels, width), jnp.bfloat16),
            pltpu.VMEM((2, 32, width), jnp.float32),
        ],
        compiler_params=pltpu.CompilerParams(vmem_limit_bytes=48 * 2**20),
        name="synth",
    )(own, halo, taps)


def added(*terms):
    return sum(term.astype(jnp.float32) for term in terms).astype(jnp.bfloat16)


def on_device(voltages, feed_position, beam_steering, synthesis_taps):
    devices = lax.axis_size("chan")
    steps = lax.axis_size("tm")
    taps = synthesis_taps.shape[0]
    feeds = voltages.shape[2]
    position = feed_position.T
    if feeds % LANES:
        position = lax.dynamic_slice_in_dim(position, lax.axis_index("chan") * feeds, feeds, 1)
    keep, send = beamform(voltages, position, beam_steering.T, devices, 0, voltages.shape[3])
    mask = 1
    while True:
        arrived = lax.ppermute(send, "chan", [(i, i ^ mask) for i in range(devices)])
        mask *= 2
        if mask == devices:
            break
        send = added(keep[1::2], arrived[1::2])
        keep = added(keep[0::2], arrived[0::2])
    own = added(keep[0], arrived[0])
    halo = lax.ppermute(own[own.shape[0] - (taps - 1) :], "tm", [(i, i + 1) for i in range(steps - 1)])
    out = synthesize(own, halo, synthesis_taps)
    return jnp.transpose(out, (0, 2, 1, 3))


def solution(mesh):
    return jax.shard_map(
        on_device,
        mesh=mesh,
        in_specs=(P(None, ("group", "tm"), "chan", None), P(), P("group", None), P()),
        out_specs=P(None, "chan", ("group", "tm"), None),
        check_vma=False,
    )
```

```python
import functools
import math

import jax
import jax.numpy as jnp
from jax import lax
from jax.experimental import pallas as pl
from jax.experimental.pallas import tpu as pltpu
from jax.sharding import PartitionSpec as P


PHASES = 4096
LANES = 128
HALF = 32
SLAB = 16
TABLE = jnp.float32


def turn(phase, steps):
    quarter = steps // 4
    shift = quarter.bit_length() - 1
    quadrant = lax.shift_right_logical(phase + quarter // 2, shift)
    rest = (phase - lax.shift_left(quadrant, shift)).astype(jnp.float32) * (2.0 * math.pi / steps)
    square = rest * rest
    sine = rest * (1.0 + square * (-1.6666666e-1 + square * (8.3333310e-3 + square * (-1.9840874e-4 + square * 2.7525562e-6))))
    cosine = 1.0 + square * (-0.5 + square * (4.1666666e-2 + square * (-1.3888889e-3 + square * (2.4801587e-5 - square * 2.7557319e-7))))
    odd = (quadrant & 1) == 1
    real = jnp.where(odd, sine, cosine)
    imag = jnp.where(odd, cosine, sine)
    real = jnp.where(((quadrant + 1) & 2) == 2, -real, real)
    imag = jnp.where((quadrant & 2) == 2, -imag, imag)
    return real, imag


def times(a, b):
    return a[0] * b[0] - a[1] * b[1], a[0] * b[1] + a[1] * b[0]


def beam_kernel(first, position_hbm, steering_hbm, voltages, keep, send, position, steering, small_arrivals, staged, arrivals, centre_tables, offset_tables, rows_even, rows_odd, sums_even, sums_odd):
    feeds, beams = offset_tables.shape[2:]
    frames = voltages.shape[1]
    stride = 2 * frames
    block = rows_even.shape[1] // stride
    devices = 2 * keep.shape[0]
    own_beams = beams // devices
    centres = centre_tables.shape[1]
    blocks = staged.shape[0]
    here = lax.axis_index("chan")
    rows_of = (rows_even, rows_odd)
    sums_of = (sums_even, sums_odd)

    def arrival(index):
        source = voltages.at[:, :, :, pl.ds(first + index * block, block)]
        return pltpu.make_async_copy(source, staged.at[index], arrivals.at[index])

    position_copy = pltpu.make_async_copy(position_hbm, position, small_arrivals.at[0])
    steering_copy = pltpu.make_async_copy(steering_hbm, steering, small_arrivals.at[1])
    position_copy.start()
    steering_copy.start()
    for index in range(blocks):
        arrival(index).start()
    position_copy.wait()
    steering_copy.wait()

    def column(axis):
        start = here * feeds if position.shape[1] > feeds else 0
        row = position[axis : axis + 1, pl.ds(pl.multiple_of(start, LANES), feeds)].astype(jnp.float32)
        return jnp.transpose(jnp.broadcast_to(row, (beams, feeds))).astype(jnp.int32)

    lane = lax.broadcasted_iota(jnp.int32, steering.shape, 1)
    aim = steering[...]
    size = own_beams
    while size < beams:
        upper = (lane & size) != 0
        swapped = jnp.where(upper, pltpu.roll(aim, size, 1), pltpu.roll(aim, beams - size, 1))
        aim = jnp.where((here & (size // own_beams)) != 0, swapped, aim)
        size *= 2
    total = column(0) * aim[0:1, :] + column(1) * aim[1:2, :]
    offset_tables[0, 0] = (total & (PHASES - 1)).astype(TABLE)

    def one_slab(index, carry):
        at = pl.multiple_of(index * SLAB, SLAB)
        delay = offset_tables[0, 0, pl.ds(at, SLAB), :].astype(jnp.int32)
        half_step = turn(delay, 2 * PHASES)
        state = half_step
        advance = times(half_step, half_step)
        for offset in range(HALF):
            offset_tables[0, offset, pl.ds(at, SLAB), :] = state[0].astype(TABLE)
            offset_tables[1, offset, pl.ds(at, SLAB), :] = state[1].astype(TABLE)
            if offset + 1 < HALF:
                state = times(state, advance)
        state = turn(((2 * first + 2 * HALF - 1) * delay) & (2 * PHASES - 1), 2 * PHASES)
        advance = turn((4 * HALF * delay) & (2 * PHASES - 1), 2 * PHASES)
        for centre in range(centres):
            centre_tables[0, centre, pl.ds(at, SLAB), :] = state[0].astype(TABLE)
            centre_tables[1, centre, pl.ds(at, SLAB), :] = state[1].astype(TABLE)
            if centre + 1 < centres:
                state = times(state, advance)
        return carry

    lax.fori_loop(0, feeds // SLAB, one_slab, 0)
    for index in range(blocks):
        arrival(index).wait()

    width = min(feeds, LANES)
    scale = 1.0 / math.sqrt(feeds * devices)
    sign = jnp.where(lax.broadcasted_iota(jnp.int32, (stride, beams), 0) < frames, -1.0, 1.0)

    def take(index, rows, slot):
        for at in range(feeds // width):
            piece = staged[index, slot // frames, slot % frames, at * width : (at + 1) * width, :].astype(jnp.float32)
            if width < LANES:
                piece = jnp.concatenate([piece, jnp.zeros((LANES - width, block), jnp.float32)], axis=0)
            rows[at, pl.ds(slot, block, stride=stride), :] = jnp.transpose(piece)

    def give(index, sums, slot):
        piece = jnp.transpose(sums[pl.ds(slot, block, stride=stride), :] * scale)
        for relative in range(devices):
            value = piece[relative * own_beams : (relative + 1) * own_beams, :].astype(jnp.bfloat16)
            out = send if relative % 2 else keep
            out[relative // 2, slot % frames, slot // frames, :, pl.ds(pl.multiple_of(index * block, block), block)] = value

    def quarter_turn(value):
        return pltpu.roll(value, frames, 0) * sign

    def dot(a, b):
        return jnp.dot(a, b, preferred_element_type=jnp.float32)

    def pair(rows, sums, cosine, sine, local, offset):
        upper = local * 2 * HALF + HALF + offset
        lower = local * 2 * HALF + HALF - 1 - offset
        pieces = []
        for at in range(feeds // width):
            top = rows[at, upper * stride : (upper + 1) * stride, :]
            bottom = rows[at, lower * stride : (lower + 1) * stride, :]
            pieces.append(jnp.concatenate([top, bottom], axis=0))
        left = jnp.concatenate(pieces, axis=1).astype(jnp.bfloat16)[:, :feeds]
        small_cosine = offset_tables[0, offset].astype(jnp.bfloat16)
        small_sine = offset_tables[1, offset].astype(jnp.bfloat16)
        straight = dot(left, jnp.concatenate([cosine * small_cosine, sine * small_sine], axis=1))
        crossed = dot(left, jnp.concatenate([sine * small_cosine, cosine * small_sine], axis=1))
        a, b, c, d = straight[:, :beams], straight[:, beams:], crossed[:, :beams], crossed[:, beams:]
        more = quarter_turn(c[:stride] + d[:stride])
        less = quarter_turn(c[stride:] - d[stride:])
        sums[upper * stride : (upper + 1) * stride, :] = a[:stride] - b[:stride] + more
        sums[lower * stride : (lower + 1) * stride, :] = a[stride:] + b[stride:] + less

    def one_block(index, parity):
        rows, sums = rows_of[parity], sums_of[parity]
        every = HALF * (block // (2 * HALF)) // stride
        for local in range(block // (2 * HALF)):
            centre = index * (block // (2 * HALF)) + local
            cosine = centre_tables[0, centre].astype(jnp.bfloat16)
            sine = centre_tables[1, centre].astype(jnp.bfloat16)
            for offset in range(HALF):
                count = local * HALF + offset
                if count % every == 0:
                    give(jnp.maximum(index - 1, 0), sums_of[1 - parity], count // every)
                    take(jnp.minimum(index + 1, blocks - 1), rows_of[1 - parity], count // every)
                pair(rows, sums, cosine, sine, local, offset)

    for slot in range(stride):
        take(0, rows_even, slot)

    def two_blocks(index, carry):
        one_block(2 * index, 0)
        one_block(2 * index + 1, 1)
        return carry

    lax.fori_loop(0, blocks // 2, two_blocks, 0)
    for slot in range(stride):
        give(blocks - 1, sums_odd, slot)


def beamform(voltages, position, steering, devices, first, count):
    _, frames, feeds, _ = voltages.shape
    beams = steering.shape[1]
    width = min(feeds, LANES)
    shape = jax.ShapeDtypeStruct((devices // 2, frames, 2, beams // devices, count), jnp.bfloat16)
    rows = pltpu.VMEM((feeds // width, LANES * 2 * frames, LANES), jnp.float32)
    sums = pltpu.VMEM((LANES * 2 * frames, beams), jnp.float32)
    work = 2 * frames * 2 * feeds * beams * count
    whole = pl.BlockSpec(memory_space=pltpu.VMEM)
    anywhere = pl.BlockSpec(memory_space=pltpu.HBM)
    return pl.pallas_call(
        functools.partial(beam_kernel, first),
        in_specs=[anywhere, anywhere, anywhere],
        out_specs=[whole, whole],
        out_shape=[shape, shape],
        scratch_shapes=[
            pltpu.VMEM(position.shape, jnp.int32),
            pltpu.VMEM(steering.shape, jnp.int32),
            pltpu.SemaphoreType.DMA((2,)),
            pltpu.VMEM((count // LANES, 2, frames, feeds, LANES), jnp.bfloat16),
            pltpu.SemaphoreType.DMA((count // LANES,)),
            pltpu.VMEM((2, count // (2 * HALF), feeds, beams), TABLE),
            pltpu.VMEM((2, HALF, feeds, beams), TABLE),
            rows,
            rows,
            sums,
            sums,
        ],
        compiler_params=pltpu.CompilerParams(vmem_limit_bytes=48 * 2**20),
        cost_estimate=pl.CostEstimate(flops=32 * work, bytes_accessed=4 * 2 * frames * feeds * count, transcendentals=0),
        name="beam",
    )(position, steering, voltages)


def basis_kernel(basis, small):
    channels = basis.shape[0]
    width = small.shape[2]
    group = small.shape[1]

    def one_slab(index, carry):
        first = pl.multiple_of(index * width, width)

        def phases(rows, factor):
            row = lax.broadcasted_iota(jnp.int32, (rows, width), 0) * factor
            column = first + lax.broadcasted_iota(jnp.int32, (rows, width), 1)
            return (row * column) & (channels - 1)

        small[0], small[1] = turn(phases(group, 1), channels)
        count = channels // group
        large = turn(phases(count, group), channels)
        for at in range(count):
            real, imag = times((large[0][at : at + 1], large[1][at : at + 1]), (small[0], small[1]))
            basis[at * group : (at + 1) * group, pl.ds(first, width)] = real.astype(jnp.bfloat16)
            basis[at * group : (at + 1) * group, pl.ds(pl.multiple_of(channels + first, width), width)] = imag.astype(jnp.bfloat16)
        return carry

    lax.fori_loop(0, channels // width, one_slab, 0)


def make_basis(channels):
    return pl.pallas_call(
        basis_kernel,
        out_specs=pl.BlockSpec(memory_space=pltpu.VMEM),
        out_shape=jax.ShapeDtypeStruct((channels, 2 * channels), jnp.bfloat16),
        scratch_shapes=[pltpu.VMEM((2, 32, 256), jnp.float32)],
        compiler_params=pltpu.CompilerParams(vmem_limit_bytes=8 * 2**20),
        cost_estimate=pl.CostEstimate(flops=2**30, bytes_accessed=4 * channels * channels, transcendentals=0),
        name="basis",
    )()


def transform(pieces, basis, first, width):
    frames, _, beams, _ = pieces[0].shape
    channels = basis.shape[0]
    total = None
    start = 0
    for piece in pieces:
        count = piece.shape[3]
        rows = [piece[t, part] for part in range(2) for t in range(frames)]
        rows = jnp.concatenate(rows, axis=0)
        for part in range(2):
            columns = pl.ds(pl.multiple_of(part * channels + first, width), width)
            product = jnp.dot(rows, basis[start : start + count, columns], preferred_element_type=jnp.float32)
            total = [None, None] if total is None else total
            total[part] = product if total[part] is None else total[part] + product
        start += count
    half = frames * beams
    scale = 1.0 / math.sqrt(channels)
    real = (total[0][:half] - total[1][half:]) * scale
    imag = (total[1][:half] + total[0][half:]) * scale
    return real.astype(jnp.bfloat16), imag.astype(jnp.bfloat16)


def frames_kernel(*refs):
    pieces, basis, out = refs[:-2], refs[-2], refs[-1]
    width = min(256, out.shape[2])

    def one_slab(index, carry):
        first = pl.multiple_of(index * width, width)
        real, imag = transform(pieces, basis, first, width)
        out[0, :, pl.ds(first, width)] = real
        out[1, :, pl.ds(first, width)] = imag
        return carry

    lax.fori_loop(0, out.shape[2] // width, one_slab, 0)


def make_frames(pieces, basis):
    frames, _, beams, _ = pieces[0].shape
    channels = basis.shape[0]
    whole = pl.BlockSpec(memory_space=pltpu.VMEM)
    return pl.pallas_call(
        frames_kernel,
        in_specs=[whole] * (len(pieces) + 1),
        out_specs=whole,
        out_shape=jax.ShapeDtypeStruct((2, frames * beams, channels), jnp.bfloat16),
        compiler_params=pltpu.CompilerParams(vmem_limit_bytes=16 * 2**20),
        cost_estimate=pl.CostEstimate(flops=8 * frames * beams * channels**2, bytes_accessed=4 * channels * channels, transcendentals=0),
        name="frames",
    )(*pieces, basis)


def taps_kernel(*refs):
    halos, own, basis, taps, out = refs[:-4], refs[-4], refs[-3], refs[-2], refs[-1]
    before, _, beams, _ = halos[0].shape
    frames = own.shape[1] // beams
    width = min(256, own.shape[2])

    def one_slab(index, carry):
        first = pl.multiple_of(index * width, width)
        earlier = transform(halos, basis, first, width)
        for part in range(2):
            rows = [earlier[part][t * beams : (t + 1) * beams].astype(jnp.float32) for t in range(before)]
            rows += [own[part, t * beams : (t + 1) * beams, pl.ds(first, width)].astype(jnp.float32) for t in range(frames)]
            for t in range(frames):
                value = jnp.zeros((beams, width), jnp.float32)
                for k in range(taps.shape[0]):
                    value = value + taps[k : k + 1, pl.ds(first, width)] * rows[before + t - k]
                out[part, t, :, pl.ds(first, width)] = value.astype(jnp.bfloat16)
        return carry

    lax.fori_loop(0, own.shape[2] // width, one_slab, 0)


def apply_taps(halos, own, basis, taps):
    before, _, beams, _ = halos[0].shape
    channels = basis.shape[0]
    frames = own.shape[1] // beams
    whole = pl.BlockSpec(memory_space=pltpu.VMEM)
    return pl.pallas_call(
        taps_kernel,
        in_specs=[whole] * (len(halos) + 3),
        out_specs=whole,
        out_shape=jax.ShapeDtypeStruct((2, frames, beams, channels), jnp.bfloat16),
        compiler_params=pltpu.CompilerParams(vmem_limit_bytes=16 * 2**20),
        cost_estimate=pl.CostEstimate(flops=8 * before * beams * channels**2, bytes_accessed=4 * channels * channels, transcendentals=0),
        name="taps",
    )(*halos, own, basis, taps)


def added(*terms):
    return sum(term.astype(jnp.float32) for term in terms).astype(jnp.bfloat16)


def steps_on_device(voltages, feed_position, beam_steering, synthesis_taps):
    devices = lax.axis_size("chan")
    steps = lax.axis_size("tm")
    taps = synthesis_taps.shape[0]
    feeds = voltages.shape[2]
    position = feed_position.T
    if feeds % LANES:
        position = lax.dynamic_slice_in_dim(position, lax.axis_index("chan") * feeds, feeds, 1)
    channels = voltages.shape[3]
    parts = [(0, channels - channels // 4), (channels - channels // 4, channels // 4)]
    basis = make_basis(channels)
    steering = beam_steering.T
    owns = []
    halos = []

    def across(value, mask):
        return lax.ppermute(value, "chan", [(i, i ^ mask) for i in range(devices)])

    def last_stage(keep, send):
        terms = [keep]
        mask = 1
        while 2 * mask < devices:
            terms.append(across(send, mask))
            send = added(*[term[1::2] for term in terms])
            terms = [term[0::2] for term in terms]
            mask *= 2
        return send, terms, mask

    def ended(terms, arrived):
        own = added(*[term[0] for term in terms], arrived[0])
        return own, lax.ppermute(own[own.shape[0] - (taps - 1) :], "tm", [(i, i + 1) for i in range(steps - 1)])

    waiting = None
    voltages = pltpu.with_memory_space_constraint(voltages, pltpu.HBM)
    for part in parts:
        keep, send = beamform(voltages, position, steering, devices, *part)
        send, terms, mask = last_stage(keep, send)
        if waiting is not None:
            arrived, send = lax.optimization_barrier((waiting[1], send))
            own, halo = ended(waiting[0], arrived)
            owns.append(own)
            halos.append(halo)
        position, send = lax.optimization_barrier((position, send))
        waiting = (terms, across(send, mask))
    own, halo = ended(*waiting)
    owns.append(own)
    halos.append(halo)
    frames = make_frames(owns, basis)
    out = apply_taps(halos, frames, basis, synthesis_taps)
    return jnp.transpose(out, (0, 2, 1, 3))


def solution(mesh):
    return jax.shard_map(
        steps_on_device,
        mesh=mesh,
        in_specs=(P(None, ("group", "tm"), "chan", None), P(), P("group", None), P()),
        out_specs=P(None, "chan", ("group", "tm"), None),
        check_vma=False,
    )
```

```python
import functools
import math

import jax
import jax.numpy as jnp
from jax import lax
from jax.experimental import pallas as pl
from jax.experimental.pallas import tpu as pltpu
from jax.sharding import PartitionSpec as P


PHASES = 4096
LANES = 128
HALF = 32
SLAB = 16
TABLE = jnp.float32
BEAM_LIMIT = 24
AHEAD = 2


def turn(phase, steps):
    quarter = steps // 4
    shift = quarter.bit_length() - 1
    quadrant = lax.shift_right_logical(phase + quarter // 2, shift)
    rest = (phase - lax.shift_left(quadrant, shift)).astype(jnp.float32) * (2.0 * math.pi / steps)
    square = rest * rest
    sine = rest * (1.0 + square * (-1.6666666e-1 + square * (8.3333310e-3 + square * (-1.9840874e-4 + square * 2.7525562e-6))))
    cosine = 1.0 + square * (-0.5 + square * (4.1666666e-2 + square * (-1.3888889e-3 + square * (2.4801587e-5 - square * 2.7557319e-7))))
    odd = (quadrant & 1) == 1
    real = jnp.where(odd, sine, cosine)
    imag = jnp.where(odd, cosine, sine)
    real = jnp.where(((quadrant + 1) & 2) == 2, -real, real)
    imag = jnp.where((quadrant & 2) == 2, -imag, imag)
    return real, imag


def times(a, b):
    return a[0] * b[0] - a[1] * b[1], a[0] * b[1] + a[1] * b[0]


def table_kernel_part(copy, position_hbm, steering_hbm, position, steering, small_arrivals, offset_tables, centre_tables, own_beams):
    feeds, beams = offset_tables.shape[2:]
    centres = centre_tables.shape[1]
    here = lax.axis_index("chan")
    position_copy = pltpu.make_async_copy(position_hbm, position, small_arrivals.at[0])
    steering_copy = pltpu.make_async_copy(steering_hbm, steering, small_arrivals.at[1])
    position_copy.start()
    steering_copy.start()
    copy.start()
    position_copy.wait()
    steering_copy.wait()

    def column(axis):
        start = here * feeds if position.shape[1] > feeds else 0
        row = position[axis : axis + 1, pl.ds(pl.multiple_of(start, LANES), feeds)].astype(jnp.float32)
        return jnp.transpose(jnp.broadcast_to(row, (beams, feeds))).astype(jnp.int32)

    lane = lax.broadcasted_iota(jnp.int32, steering.shape, 1)
    aim = steering[...]
    size = own_beams
    while size < beams:
        upper = (lane & size) != 0
        swapped = jnp.where(upper, pltpu.roll(aim, size, 1), pltpu.roll(aim, beams - size, 1))
        aim = jnp.where((here & (size // own_beams)) != 0, swapped, aim)
        size *= 2
    total = column(0) * aim[0:1, :] + column(1) * aim[1:2, :]
    offset_tables[0, 0] = (total & (PHASES - 1)).astype(TABLE)

    def one_slab(index, carry):
        at = pl.multiple_of(index * SLAB, SLAB)
        delay = offset_tables[0, 0, pl.ds(at, SLAB), :].astype(jnp.int32)
        half_step = turn(delay, 2 * PHASES)
        state = half_step
        advance = times(half_step, half_step)
        for offset in range(HALF):
            offset_tables[0, offset, pl.ds(at, SLAB), :] = state[0].astype(TABLE)
            offset_tables[1, offset, pl.ds(at, SLAB), :] = state[1].astype(TABLE)
            if offset + 1 < HALF:
                state = times(state, advance)
        state = turn(((2 * HALF - 1) * delay) & (2 * PHASES - 1), 2 * PHASES)
        advance = turn((4 * HALF * delay) & (2 * PHASES - 1), 2 * PHASES)
        for centre in range(centres):
            centre_tables[0, centre, pl.ds(at, SLAB), :] = state[0].astype(TABLE)
            centre_tables[1, centre, pl.ds(at, SLAB), :] = state[1].astype(TABLE)
            if centre + 1 < centres:
                state = times(state, advance)
        return carry

    lax.fori_loop(0, feeds // SLAB, one_slab, 0)


def beam_kernel(first, make_tables, *refs):
    if make_tables:
        position_hbm, steering_hbm, voltages, keep, send, offset_tables, centre_tables, staged = refs[:8]
        position, steering, small_arrivals, arrivals = refs[8:12]
    else:
        offset_tables, centre_tables, staged, keep, send = refs[:5]
    both_rows, both_sums = refs[-2:]
    feeds, beams = offset_tables.shape[2:]
    frames = staged.shape[1]
    stride = 2 * frames
    block = LANES
    devices = 2 * keep.shape[0]
    own_beams = beams // devices
    before = first // block
    blocks = keep.shape[4] // block

    if make_tables:
        copy = pltpu.make_async_copy(voltages, staged, arrivals.at[0])
        table_kernel_part(copy, position_hbm, steering_hbm, position, steering, small_arrivals, offset_tables, centre_tables, own_beams)
        copy.wait()

    width = min(feeds, LANES)
    scale = 1.0 / math.sqrt(feeds * devices)
    sign = jnp.where(lax.broadcasted_iota(jnp.int32, (stride, beams), 0) < frames, -1.0, 1.0)

    def take(index, rows, slot):
        for at in range(feeds // width):
            lanes = pl.ds(pl.multiple_of((before + index) * block, block), block)
            piece = staged[slot // frames, slot % frames, at * width : (at + 1) * width, lanes].astype(jnp.float32)
            if width < LANES:
                piece = jnp.concatenate([piece, jnp.zeros((LANES - width, block), jnp.float32)], axis=0)
            rows[at, pl.ds(slot, block, stride=stride), :] = jnp.transpose(piece)

    def give(index, sums, slot):
        piece = jnp.transpose(sums[pl.ds(slot, block, stride=stride), :] * scale)
        for relative in range(devices):
            value = piece[relative * own_beams : (relative + 1) * own_beams, :].astype(jnp.bfloat16)
            out = send if relative % 2 else keep
            out[relative // 2, slot % frames, slot // frames, :, pl.ds(pl.multiple_of(index * block, block), block)] = value

    def quarter_turn(value):
        return pltpu.roll(value, frames, 0) * sign

    def dot(a, b):
        return jnp.dot(a, b, preferred_element_type=jnp.float32)

    def lhs(rows, local, offset):
        upper = local * 2 * HALF + HALF + offset
        lower = local * 2 * HALF + HALF - 1 - offset
        pieces = []
        for at in range(feeds // width):
            top = rows[at, upper * stride : (upper + 1) * stride, :]
            bottom = rows[at, lower * stride : (lower + 1) * stride, :]
            pieces.append(jnp.concatenate([top, bottom], axis=0))
        return jnp.concatenate(pieces, axis=1).astype(jnp.bfloat16)[:, :feeds]

    def pair(left, sums, cosine, sine, local, offset):
        upper = local * 2 * HALF + HALF + offset
        lower = local * 2 * HALF + HALF - 1 - offset
        small_cosine = offset_tables[0, offset].astype(jnp.bfloat16)
        small_sine = offset_tables[1, offset].astype(jnp.bfloat16)
        straight = dot(left, jnp.concatenate([cosine * small_cosine, sine * small_sine], axis=1))
        crossed = dot(left, jnp.concatenate([sine * small_cosine, cosine * small_sine], axis=1))
        a, b, c, d = straight[:, :beams], straight[:, beams:], crossed[:, :beams], crossed[:, beams:]
        more = quarter_turn(c[:stride] + d[:stride])
        less = quarter_turn(c[stride:] - d[stride:])
        sums[upper * stride : (upper + 1) * stride, :] = a[:stride] - b[:stride] + more
        sums[lower * stride : (lower + 1) * stride, :] = a[stride:] + b[stride:] + less

    def one_block(index, parity):
        rows, sums = both_rows.at[parity], both_sums.at[parity]
        other_rows, other_sums = both_rows.at[1 - parity], both_sums.at[1 - parity]
        locals_ = block // (2 * HALF)
        every = HALF * locals_ // stride
        lefts = [(local, offset) for local in range(locals_) for offset in range(HALF)]
        ready = [lhs(rows, *at) for at in lefts[:AHEAD]]
        for count, (local, offset) in enumerate(lefts):
            if offset == 0:
                centre = (before + index) * locals_ + local
                cosine = centre_tables[0, centre].astype(jnp.bfloat16)
                sine = centre_tables[1, centre].astype(jnp.bfloat16)
            if count % every == 0:
                give(jnp.maximum(index - 1, 0), other_sums, count // every)
                take(jnp.minimum(index + 1, blocks - 1), other_rows, count // every)
            if count + AHEAD < len(lefts):
                ready.append(lhs(rows, *lefts[count + AHEAD]))
            pair(ready[count], sums, cosine, sine, local, offset)

    for slot in range(stride):
        take(0, both_rows.at[0], slot)

    def two_blocks(index, carry):
        one_block(2 * index, 0)
        one_block(2 * index + 1, 1)
        return carry

    lax.fori_loop(0, blocks // 2, two_blocks, 0)
    if blocks % 2:
        one_block(blocks - 1, 0)
    for slot in range(stride):
        give(blocks - 1, both_sums.at[(blocks - 1) & 1], slot)


def beamform(voltages, position, steering, devices, first, count, tables):
    _, frames, feeds, channels = voltages.shape
    beams = steering.shape[1]
    width = min(feeds, LANES)
    shape = jax.ShapeDtypeStruct((devices // 2, frames, 2, beams // devices, count), jnp.bfloat16)
    rows = pltpu.VMEM((2, feeds // width, LANES * 2 * frames, LANES), jnp.float32)
    sums = pltpu.VMEM((2, LANES * 2 * frames, beams), jnp.float32)
    work = 2 * frames * 2 * feeds * beams * count
    whole = pl.BlockSpec(memory_space=pltpu.VMEM)
    anywhere = pl.BlockSpec(memory_space=pltpu.HBM)
    out_shape = [shape, shape]
    scratch = []
    if tables is None:
        out_shape += [
            jax.ShapeDtypeStruct((2, HALF, feeds, beams), TABLE),
            jax.ShapeDtypeStruct((2, channels // (2 * HALF), feeds, beams), TABLE),
            jax.ShapeDtypeStruct(voltages.shape, jnp.bfloat16),
        ]
        scratch += [
            pltpu.VMEM(position.shape, jnp.int32),
            pltpu.VMEM(steering.shape, jnp.int32),
            pltpu.SemaphoreType.DMA((2,)),
            pltpu.SemaphoreType.DMA((1,)),
        ]
        position = pltpu.with_memory_space_constraint(position, pltpu.HBM)
        steering = pltpu.with_memory_space_constraint(steering, pltpu.HBM)
        args, in_specs = (position, steering, voltages), [anywhere] * 3
    else:
        args, in_specs = tables, [whole] * 3
    out = pl.pallas_call(
        functools.partial(beam_kernel, first, tables is None),
        in_specs=in_specs,
        out_specs=[whole] * len(out_shape),
        out_shape=out_shape,
        scratch_shapes=scratch
        + [rows, sums],
        compiler_params=pltpu.CompilerParams(vmem_limit_bytes=BEAM_LIMIT * 2**20),
        cost_estimate=pl.CostEstimate(flops=32 * work, bytes_accessed=4 * 2 * frames * feeds * count, transcendentals=0),
        name="beam",
    )(*args)
    return out[0], out[1], out[2:] if tables is None else tables


def basis_kernel(basis, small):
    channels = basis.shape[0]
    width = small.shape[2]
    group = small.shape[1]

    def one_slab(index, carry):
        first = pl.multiple_of(index * width, width)

        def phases(rows, factor):
            row = lax.broadcasted_iota(jnp.int32, (rows, width), 0) * factor
            column = first + lax.broadcasted_iota(jnp.int32, (rows, width), 1)
            return (row * column) & (channels - 1)

        small[0], small[1] = turn(phases(group, 1), channels)
        count = channels // group
        large = turn(phases(count, group), channels)
        for at in range(count):
            real, imag = times((large[0][at : at + 1], large[1][at : at + 1]), (small[0], small[1]))
            basis[at * group : (at + 1) * group, pl.ds(first, width)] = real.astype(jnp.bfloat16)
            basis[at * group : (at + 1) * group, pl.ds(pl.multiple_of(channels + first, width), width)] = imag.astype(jnp.bfloat16)
        return carry

    lax.fori_loop(0, channels // width, one_slab, 0)


def make_basis(channels):
    return pl.pallas_call(
        basis_kernel,
        out_specs=pl.BlockSpec(memory_space=pltpu.VMEM),
        out_shape=jax.ShapeDtypeStruct((channels, 2 * channels), jnp.bfloat16),
        scratch_shapes=[pltpu.VMEM((2, 32, 256), jnp.float32)],
        compiler_params=pltpu.CompilerParams(vmem_limit_bytes=8 * 2**20),
        cost_estimate=pl.CostEstimate(flops=2**30, bytes_accessed=4 * channels * channels, transcendentals=0),
        name="basis",
    )()


def transform(pieces, starts, basis, first, width):
    frames, _, beams, _ = pieces[0].shape
    channels = basis.shape[0]
    total = None
    for piece, start in zip(pieces, starts):
        count = piece.shape[3]
        rows = jnp.concatenate([piece[t, part] for part in range(2) for t in range(frames)], axis=0)
        for part in range(2):
            columns = pl.ds(pl.multiple_of(part * channels + first, width), width)
            product = jnp.dot(rows, basis[start : start + count, columns], preferred_element_type=jnp.float32)
            total = [None, None] if total is None else total
            total[part] = product if total[part] is None else total[part] + product
    half = frames * beams
    return total[0][:half] - total[1][half:], total[1][:half] + total[0][half:]


def own_kernel(starts, *refs):
    pieces, basis, taps, out = refs[:-3], refs[-3], refs[-2], refs[-1]
    frames, _, beams, _ = pieces[0].shape
    channels = basis.shape[0]
    width = min(256, channels)
    scale = 1.0 / math.sqrt(channels)

    def one_slab(index, carry):
        first = pl.multiple_of(index * width, width)
        for part, value in enumerate(transform(pieces, starts, basis, first, width)):
            value = (value * scale).astype(jnp.bfloat16).astype(jnp.float32)
            for t in range(frames):
                total = None
                for k in range(min(t + 1, taps.shape[0])):
                    term = taps[k : k + 1, pl.ds(first, width)] * value[(t - k) * beams : (t - k + 1) * beams]
                    total = term if total is None else total + term
                out[part, t, :, pl.ds(first, width)] = total
        return carry

    lax.fori_loop(0, channels // width, one_slab, 0)


def halo_kernel(starts, *refs):
    pieces, basis, out = refs[:-2], refs[-2], refs[-1]
    channels = basis.shape[0]
    width = min(256, channels)

    def one_slab(index, carry):
        first = pl.multiple_of(index * width, width)
        for part, value in enumerate(transform(pieces, starts, basis, first, width)):
            out[part, :, pl.ds(first, width)] = value
        return carry

    lax.fori_loop(0, channels // width, one_slab, 0)


def taps_kernel(starts, *refs):
    pieces, others, own, basis, taps, out, turned = refs[:-6], refs[-6], refs[-5], refs[-4], refs[-3], refs[-2], refs[-1]
    before, _, beams, _ = pieces[0].shape
    channels = basis.shape[0]
    frames = own.shape[1]
    width = min(256, channels)
    scale = 1.0 / math.sqrt(channels)

    def one_slab(index, carry):
        first = pl.multiple_of(index * width, width)
        lanes = pl.ds(first, width)
        for part, value in enumerate(transform(pieces, starts, basis, first, width)):
            value = ((value + others[part, :, lanes]) * scale).astype(jnp.bfloat16).astype(jnp.float32)
            for t in range(frames):
                total = own[part, t, :, lanes]
                for k in range(t + 1, taps.shape[0]):
                    at = before + t - k
                    total = total + taps[k : k + 1, lanes] * value[at * beams : (at + 1) * beams]
                for at in range(width // LANES):
                    turned[part, at, pl.ds(t, beams, stride=frames), :] = total[:, at * LANES : (at + 1) * LANES]
            for at in range(width // LANES):
                start = pl.multiple_of(first + at * LANES, LANES)
                out[part, :, :, pl.ds(start, LANES)] = turned[part, at].reshape(beams, frames, LANES).astype(jnp.bfloat16)
        return carry

    lax.fori_loop(0, channels // width, one_slab, 0)


def small_call(kernel, rows, args, out_shape, scratch=()):
    channels = out_shape.shape[-1]
    whole = pl.BlockSpec(memory_space=pltpu.VMEM)
    return pl.pallas_call(
        kernel,
        in_specs=[whole] * len(args),
        out_specs=whole,
        out_shape=out_shape,
        scratch_shapes=scratch,
        compiler_params=pltpu.CompilerParams(vmem_limit_bytes=12 * 2**20),
        cost_estimate=pl.CostEstimate(flops=8 * rows * channels**2, bytes_accessed=4 * channels**2, transcendentals=0),
    )(*args)


def added(*terms):
    return sum(term.astype(jnp.float32) for term in terms).astype(jnp.bfloat16)


def steps_on_device(voltages, feed_position, beam_steering, synthesis_taps):
    devices = lax.axis_size("chan")
    steps = lax.axis_size("tm")
    taps = synthesis_taps.shape[0]
    feeds = voltages.shape[2]
    position = feed_position.T
    if feeds % LANES:
        position = lax.dynamic_slice_in_dim(position, lax.axis_index("chan") * feeds, feeds, 1)
    channels = voltages.shape[3]
    later = max(1, 3 * channels // (8 * LANES)) * LANES
    parts = [(0, channels - later), (channels - later, later)]
    basis = make_basis(channels)
    steering = beam_steering.T
    owns = []
    halos = []

    def across(value, mask):
        return lax.ppermute(value, "chan", [(i, i ^ mask) for i in range(devices)])

    def last_stage(keep, send):
        terms = [keep]
        mask = 1
        while 2 * mask < devices:
            terms.append(across(send, mask))
            send = added(*[term[1::2] for term in terms])
            terms = [term[0::2] for term in terms]
            mask *= 2
        return send, terms, mask

    def ended(terms, arrived):
        own = added(*[term[0] for term in terms], arrived[0])
        return own, lax.ppermute(own[own.shape[0] - (taps - 1) :], "tm", [(i, i + 1) for i in range(steps - 1)])

    waiting = None
    voltages = pltpu.with_memory_space_constraint(voltages, pltpu.HBM)
    waiting = None
    tables = None
    for part in parts:
        if waiting is not None:
            tables, send = lax.optimization_barrier((tables, waiting[1]))
            waiting = (waiting[0], send, waiting[2])
            waiting = (waiting[0], across(*waiting[1:]))
        keep, send, tables = beamform(voltages, position, steering, devices, *part, tables)
        send, terms, mask = last_stage(keep, send)
        if waiting is not None:
            arrived, send = lax.optimization_barrier((waiting[1], send))
            own, halo = ended(waiting[0], arrived)
            owns.append(own)
            halos.append(halo)
        waiting = (terms, send, mask)
    own, halo = ended(waiting[0], across(*waiting[1:]))
    owns.append(own)
    halos.append(halo)
    starts = [start for start, _ in parts]
    frames, _, beams, _ = own.shape
    before = taps - 1
    single = jnp.float32
    sums = jax.ShapeDtypeStruct((2, frames, beams, channels), single)
    filtered = small_call(functools.partial(own_kernel, starts), frames * beams, (*owns, basis, synthesis_taps), sums)
    part_sums = jax.ShapeDtypeStruct((2, before * beams, channels), single)
    others = small_call(functools.partial(halo_kernel, starts[:-1]), before * beams, (*halos[:-1], basis), part_sums)
    out_shape = jax.ShapeDtypeStruct((2, beams, frames, channels), jnp.bfloat16)
    turned = pltpu.VMEM((2, 256 // LANES, frames * beams, LANES), single)
    args = (*halos[-1:], others, filtered, basis, synthesis_taps)
    return small_call(functools.partial(taps_kernel, starts[-1:]), before * beams, args, out_shape, [turned])


def solution(mesh):
    return jax.shard_map(
        steps_on_device,
        mesh=mesh,
        in_specs=(P(None, ("group", "tm"), "chan", None), P(), P("group", None), P()),
        out_specs=P(None, "chan", ("group", "tm"), None),
        check_vma=False,
    )
```

```python
import functools
import math

import jax
import jax.numpy as jnp
from jax import lax
from jax.experimental import pallas as pl
from jax.experimental.pallas import tpu as pltpu
from jax.sharding import PartitionSpec as P


PHASES = 4096
LANES = 128
HALF = 32
SLAB = 16
TABLE = jnp.float32
BEAM_LIMIT = 24
AHEAD = 2


def turn(phase, steps):
    quarter = steps // 4
    shift = quarter.bit_length() - 1
    quadrant = lax.shift_right_logical(phase + quarter // 2, shift)
    rest = (phase - lax.shift_left(quadrant, shift)).astype(jnp.float32) * (2.0 * math.pi / steps)
    square = rest * rest
    sine = rest * (1.0 + square * (-1.6666666e-1 + square * (8.3333310e-3 + square * (-1.9840874e-4 + square * 2.7525562e-6))))
    cosine = 1.0 + square * (-0.5 + square * (4.1666666e-2 + square * (-1.3888889e-3 + square * (2.4801587e-5 - square * 2.7557319e-7))))
    odd = (quadrant & 1) == 1
    real = jnp.where(odd, sine, cosine)
    imag = jnp.where(odd, cosine, sine)
    real = jnp.where(((quadrant + 1) & 2) == 2, -real, real)
    imag = jnp.where((quadrant & 2) == 2, -imag, imag)
    return real, imag


def times(a, b):
    return a[0] * b[0] - a[1] * b[1], a[0] * b[1] + a[1] * b[0]


def table_kernel_part(copy, position_hbm, steering_hbm, position, steering, small_arrivals, offset_tables, centre_tables, own_beams):
    feeds, beams = offset_tables.shape[2:]
    centres = centre_tables.shape[1]
    here = lax.axis_index("chan")
    position_copy = pltpu.make_async_copy(position_hbm, position, small_arrivals.at[0])
    steering_copy = pltpu.make_async_copy(steering_hbm, steering, small_arrivals.at[1])
    position_copy.start()
    steering_copy.start()
    copy.start()
    position_copy.wait()
    steering_copy.wait()

    def column(axis):
        start = here * feeds if position.shape[1] > feeds else 0
        row = position[axis : axis + 1, pl.ds(pl.multiple_of(start, LANES), feeds)].astype(jnp.float32)
        return jnp.transpose(jnp.broadcast_to(row, (beams, feeds))).astype(jnp.int32)

    lane = lax.broadcasted_iota(jnp.int32, steering.shape, 1)
    aim = steering[...]
    size = own_beams
    while size < beams:
        upper = (lane & size) != 0
        swapped = jnp.where(upper, pltpu.roll(aim, size, 1), pltpu.roll(aim, beams - size, 1))
        aim = jnp.where((here & (size // own_beams)) != 0, swapped, aim)
        size *= 2
    total = column(0) * aim[0:1, :] + column(1) * aim[1:2, :]
    offset_tables[0, 0] = (total & (PHASES - 1)).astype(TABLE)

    def one_slab(index, carry):
        at = pl.multiple_of(index * SLAB, SLAB)
        delay = offset_tables[0, 0, pl.ds(at, SLAB), :].astype(jnp.int32)
        half_step = turn(delay, 2 * PHASES)
        state = half_step
        advance = times(half_step, half_step)
        for offset in range(HALF):
            offset_tables[0, offset, pl.ds(at, SLAB), :] = state[0].astype(TABLE)
            offset_tables[1, offset, pl.ds(at, SLAB), :] = state[1].astype(TABLE)
            if offset + 1 < HALF:
                state = times(state, advance)
        state = turn(((2 * HALF - 1) * delay) & (2 * PHASES - 1), 2 * PHASES)
        advance = turn((4 * HALF * delay) & (2 * PHASES - 1), 2 * PHASES)
        for centre in range(centres):
            centre_tables[0, centre, pl.ds(at, SLAB), :] = state[0].astype(TABLE)
            centre_tables[1, centre, pl.ds(at, SLAB), :] = state[1].astype(TABLE)
            if centre + 1 < centres:
                state = times(state, advance)
        return carry

    lax.fori_loop(0, feeds // SLAB, one_slab, 0)


def beam_kernel(first, make_tables, *refs):
    if make_tables:
        position_hbm, steering_hbm, voltages, keep, send, offset_tables, centre_tables, staged = refs[:8]
        position, steering, small_arrivals, arrivals = refs[8:12]
    else:
        offset_tables, centre_tables, staged, keep, send = refs[:5]
    both_rows, both_sums = refs[-2:]
    feeds, beams = offset_tables.shape[2:]
    frames = staged.shape[1]
    stride = 2 * frames
    block = LANES
    devices = 2 * keep.shape[0]
    own_beams = beams // devices
    before = first // block
    blocks = keep.shape[4] // block

    if make_tables:
        copy = pltpu.make_async_copy(voltages, staged, arrivals.at[0])
        table_kernel_part(copy, position_hbm, steering_hbm, position, steering, small_arrivals, offset_tables, centre_tables, own_beams)
        copy.wait()

    width = min(feeds, LANES)
    scale = 1.0 / math.sqrt(feeds * devices)
    sign = jnp.where(lax.broadcasted_iota(jnp.int32, (stride, beams), 0) < frames, -1.0, 1.0)

    def take(index, rows, slot):
        for at in range(feeds // width):
            lanes = pl.ds(pl.multiple_of((before + index) * block, block), block)
            piece = staged[slot // frames, slot % frames, at * width : (at + 1) * width, lanes].astype(jnp.float32)
            if width < LANES:
                piece = jnp.concatenate([piece, jnp.zeros((LANES - width, block), jnp.float32)], axis=0)
            rows[at, pl.ds(slot, block, stride=stride), :] = jnp.transpose(piece)

    def give(index, sums, slot):
        piece = jnp.transpose(sums[pl.ds(slot, block, stride=stride), :] * scale)
        for relative in range(devices):
            value = piece[relative * own_beams : (relative + 1) * own_beams, :].astype(jnp.bfloat16)
            out = send if relative % 2 else keep
            out[relative // 2, slot % frames, slot // frames, :, pl.ds(pl.multiple_of(index * block, block), block)] = value

    def quarter_turn(value):
        return pltpu.roll(value, frames, 0) * sign

    def dot(a, b):
        return jnp.dot(a, b, preferred_element_type=jnp.float32)

    def lhs(rows, local, offset):
        upper = local * 2 * HALF + HALF + offset
        lower = local * 2 * HALF + HALF - 1 - offset
        pieces = []
        for at in range(feeds // width):
            top = rows[at, upper * stride : (upper + 1) * stride, :]
            bottom = rows[at, lower * stride : (lower + 1) * stride, :]
            pieces.append(jnp.concatenate([top, bottom], axis=0))
        return jnp.concatenate(pieces, axis=1).astype(jnp.bfloat16)[:, :feeds]

    def pair(left, sums, cosine, sine, local, offset):
        upper = local * 2 * HALF + HALF + offset
        lower = local * 2 * HALF + HALF - 1 - offset
        small_cosine = offset_tables[0, offset].astype(jnp.bfloat16)
        small_sine = offset_tables[1, offset].astype(jnp.bfloat16)
        straight = dot(left, jnp.concatenate([cosine * small_cosine, sine * small_sine], axis=1))
        crossed = dot(left, jnp.concatenate([sine * small_cosine, cosine * small_sine], axis=1))
        a, b, c, d = straight[:, :beams], straight[:, beams:], crossed[:, :beams], crossed[:, beams:]
        more = quarter_turn(c[:stride] + d[:stride])
        less = quarter_turn(c[stride:] - d[stride:])
        sums[upper * stride : (upper + 1) * stride, :] = a[:stride] - b[:stride] + more
        sums[lower * stride : (lower + 1) * stride, :] = a[stride:] + b[stride:] + less

    def one_block(index, parity):
        rows, sums = both_rows.at[parity], both_sums.at[parity]
        other_rows, other_sums = both_rows.at[1 - parity], both_sums.at[1 - parity]
        locals_ = block // (2 * HALF)
        every = HALF * locals_ // stride
        lefts = [(local, offset) for local in range(locals_) for offset in range(HALF)]
        ready = [lhs(rows, *at) for at in lefts[:AHEAD]]
        for count, (local, offset) in enumerate(lefts):
            if offset == 0:
                centre = (before + index) * locals_ + local
                cosine = centre_tables[0, centre].astype(jnp.bfloat16)
                sine = centre_tables[1, centre].astype(jnp.bfloat16)
            if count % every == 0:
                give(jnp.maximum(index - 1, 0), other_sums, count // every)
                take(jnp.minimum(index + 1, blocks - 1), other_rows, count // every)
            if count + AHEAD < len(lefts):
                ready.append(lhs(rows, *lefts[count + AHEAD]))
            pair(ready[count], sums, cosine, sine, local, offset)

    for slot in range(stride):
        take(0, both_rows.at[0], slot)

    def two_blocks(index, carry):
        one_block(2 * index, 0)
        one_block(2 * index + 1, 1)
        return carry

    lax.fori_loop(0, blocks // 2, two_blocks, 0)
    if blocks % 2:
        one_block(blocks - 1, 0)
    for slot in range(stride):
        give(blocks - 1, both_sums.at[(blocks - 1) & 1], slot)


def beamform(voltages, position, steering, devices, first, count, tables):
    _, frames, feeds, channels = voltages.shape
    beams = steering.shape[1]
    width = min(feeds, LANES)
    shape = jax.ShapeDtypeStruct((devices // 2, frames, 2, beams // devices, count), jnp.bfloat16)
    rows = pltpu.VMEM((2, feeds // width, LANES * 2 * frames, LANES), jnp.float32)
    sums = pltpu.VMEM((2, LANES * 2 * frames, beams), jnp.float32)
    work = 2 * frames * 2 * feeds * beams * count
    whole = pl.BlockSpec(memory_space=pltpu.VMEM)
    anywhere = pl.BlockSpec(memory_space=pltpu.HBM)
    out_shape = [shape, shape]
    scratch = []
    if tables is None:
        out_shape += [
            jax.ShapeDtypeStruct((2, HALF, feeds, beams), TABLE),
            jax.ShapeDtypeStruct((2, channels // (2 * HALF), feeds, beams), TABLE),
            jax.ShapeDtypeStruct(voltages.shape, jnp.bfloat16),
        ]
        scratch += [
            pltpu.VMEM(position.shape, jnp.int32),
            pltpu.VMEM(steering.shape, jnp.int32),
            pltpu.SemaphoreType.DMA((2,)),
            pltpu.SemaphoreType.DMA((1,)),
        ]
        position = pltpu.with_memory_space_constraint(position, pltpu.HBM)
        steering = pltpu.with_memory_space_constraint(steering, pltpu.HBM)
        args, in_specs = (position, steering, voltages), [anywhere] * 3
    else:
        args, in_specs = tables, [whole] * 3
    out = pl.pallas_call(
        functools.partial(beam_kernel, first, tables is None),
        in_specs=in_specs,
        out_specs=[whole] * len(out_shape),
        out_shape=out_shape,
        scratch_shapes=scratch
        + [rows, sums],
        compiler_params=pltpu.CompilerParams(vmem_limit_bytes=BEAM_LIMIT * 2**20),
        cost_estimate=pl.CostEstimate(flops=32 * work, bytes_accessed=4 * 2 * frames * feeds * count, transcendentals=0),
        name="beam",
    )(*args)
    return out[0], out[1], out[2:] if tables is None else tables


def basis_kernel(basis, small):
    channels = basis.shape[0]
    width = small.shape[2]
    group = small.shape[1]

    def one_slab(index, carry):
        first = pl.multiple_of(index * width, width)

        def phases(rows, factor):
            row = lax.broadcasted_iota(jnp.int32, (rows, width), 0) * factor
            column = first + lax.broadcasted_iota(jnp.int32, (rows, width), 1)
            return (row * column) & (channels - 1)

        small[0], small[1] = turn(phases(group, 1), channels)
        count = channels // group
        large = turn(phases(count, group), channels)
        for at in range(count):
            real, imag = times((large[0][at : at + 1], large[1][at : at + 1]), (small[0], small[1]))
            basis[at * group : (at + 1) * group, pl.ds(first, width)] = real.astype(jnp.bfloat16)
            basis[at * group : (at + 1) * group, pl.ds(pl.multiple_of(channels + first, width), width)] = imag.astype(jnp.bfloat16)
        return carry

    lax.fori_loop(0, channels // width, one_slab, 0)


def make_basis(channels):
    return pl.pallas_call(
        basis_kernel,
        out_specs=pl.BlockSpec(memory_space=pltpu.VMEM),
        out_shape=jax.ShapeDtypeStruct((channels, 2 * channels), jnp.bfloat16),
        scratch_shapes=[pltpu.VMEM((2, 32, 256), jnp.float32)],
        compiler_params=pltpu.CompilerParams(vmem_limit_bytes=8 * 2**20),
        cost_estimate=pl.CostEstimate(flops=2**30, bytes_accessed=4 * channels * channels, transcendentals=0),
        name="basis",
    )()


def transform(pieces, starts, basis, first, width):
    frames, _, beams, _ = pieces[0].shape
    channels = basis.shape[0]
    total = None
    for piece, start in zip(pieces, starts):
        count = piece.shape[3]
        rows = jnp.concatenate([piece[t, part] for part in range(2) for t in range(frames)], axis=0)
        for part in range(2):
            column = part * channels + first
            columns = pl.ds(column if isinstance(column, int) else pl.multiple_of(column, width), width)
            product = jnp.dot(rows, basis[start : start + count, columns], preferred_element_type=jnp.float32)
            total = [None, None] if total is None else total
            total[part] = product if total[part] is None else total[part] + product
    half = frames * beams
    return total[0][:half] - total[1][half:], total[1][:half] + total[0][half:]


def own_kernel(starts, *refs):
    pieces, others, basis, taps, out = refs[:-4], refs[-4], refs[-3], refs[-2], refs[-1]
    frames, _, beams, _ = pieces[0].shape
    channels = basis.shape[0]
    width = min(256, channels)
    scale = 1.0 / math.sqrt(channels)

    def one_slab(index, carry):
        first = pl.multiple_of(index * width, width)
        for part, value in enumerate(transform(pieces, starts, basis, first, width)):
            value = ((value + others[part, :, pl.ds(first, width)]) * scale).astype(jnp.bfloat16).astype(jnp.float32)
            for t in range(frames):
                total = None
                for k in range(min(t + 1, taps.shape[0])):
                    term = taps[k : k + 1, pl.ds(first, width)] * value[(t - k) * beams : (t - k + 1) * beams]
                    total = term if total is None else total + term
                out[part, t, :, pl.ds(first, width)] = total
        return carry

    lax.fori_loop(0, channels // width, one_slab, 0)


def part_kernel(starts, wraps, *refs):
    pieces, basis, out = refs[:-2], refs[-2], refs[-1]
    channels = basis.shape[0]
    width = min(256, channels)

    def one_slab(index, carry):
        first = pl.multiple_of(index * width, width)
        for part, value in enumerate(transform(pieces, starts, basis, first, width)):
            out[part, :, pl.ds(first, width)] = jnp.where(lax.axis_index("tm") == 0, 0.0, value) if wraps else value
        return carry

    lax.fori_loop(0, channels // width, one_slab, 0)


def taps_kernel(starts, *refs):
    pieces, others, own, basis, taps, out = refs[:-8], refs[-8], refs[-7], refs[-6], refs[-5], refs[-4]
    turned, result, departures = refs[-3:]
    before, _, beams, _ = pieces[0].shape
    channels = basis.shape[0]
    frames = own.shape[1]
    slabs = departures.shape[0]
    width = channels // slabs
    scale = 1.0 / math.sqrt(channels)

    def departure(index):
        lanes = pl.ds(index * width, width)
        return pltpu.make_async_copy(result.at[index], out.at[:, :, :, lanes], departures.at[index])

    for index in range(slabs):
        lanes = pl.ds(index * width, width)
        for part, value in enumerate(transform(pieces, starts, basis, index * width, width)):
            value = ((value + others[part, :, lanes]) * scale).astype(jnp.bfloat16).astype(jnp.float32)
            for t in range(frames):
                total = own[part, t, :, lanes]
                for k in range(t + 1, taps.shape[0]):
                    at = before + t - k
                    total = total + taps[k : k + 1, lanes] * value[at * beams : (at + 1) * beams]
                for at in range(width // LANES):
                    turned[index, part, at, pl.ds(t, beams, stride=frames), :] = total[:, at * LANES : (at + 1) * LANES]
            for at in range(width // LANES):
                value = turned[index, part, at].reshape(beams, frames, LANES).astype(jnp.bfloat16)
                result[index, part, :, :, at * LANES : (at + 1) * LANES] = value
        departure(index).start()
    for index in range(slabs):
        departure(index).wait()


def small_call(kernel, rows, args, out_shape, scratch=(), space=pltpu.VMEM):
    channels = out_shape.shape[-1]
    whole = pl.BlockSpec(memory_space=pltpu.VMEM)
    return pl.pallas_call(
        kernel,
        in_specs=[whole] * len(args),
        out_specs=pl.BlockSpec(memory_space=space),
        out_shape=out_shape,
        scratch_shapes=scratch,
        compiler_params=pltpu.CompilerParams(vmem_limit_bytes=12 * 2**20),
        cost_estimate=pl.CostEstimate(flops=8 * rows * channels**2, bytes_accessed=4 * channels**2, transcendentals=0),
    )(*args)


def added(*terms):
    return sum(term.astype(jnp.float32) for term in terms).astype(jnp.bfloat16)


def steps_on_device(voltages, feed_position, beam_steering, synthesis_taps):
    devices = lax.axis_size("chan")
    steps = lax.axis_size("tm")
    taps = synthesis_taps.shape[0]
    before = taps - 1
    feeds = voltages.shape[2]
    position = feed_position.T
    if feeds % LANES:
        position = lax.dynamic_slice_in_dim(position, lax.axis_index("chan") * feeds, feeds, 1)
    channels = voltages.shape[3]
    later = max(1, 3 * channels // (8 * LANES)) * LANES
    parts = [(0, channels - later), (channels - later, later)]
    basis = make_basis(channels)
    steering = beam_steering.T
    owns = []
    halos = []

    def across(value, mask):
        return lax.ppermute(value, "chan", [(i, i ^ mask) for i in range(devices)])

    def last_stage(keep, send):
        terms = [keep]
        mask = 1
        while 2 * mask < devices:
            terms.append(across(send, mask))
            send = added(*[term[1::2] for term in terms])
            terms = [term[0::2] for term in terms]
            mask *= 2
        return send, terms, mask

    def ended(terms, arrived, hops):
        own = lax.optimization_barrier(added(*[term[0] for term in terms], arrived[0]))
        return own, lax.ppermute(own[own.shape[0] - before :], "tm", hops)

    voltages = pltpu.with_memory_space_constraint(voltages, pltpu.HBM)
    split = voltages.shape[1] - before
    keep, send, tables = beamform(voltages, position, steering, devices, *parts[0], None)
    send, first_terms, mask = last_stage(keep, send)
    tables, send = lax.optimization_barrier((tables, send))
    arrived = across(send, mask)
    keep, send, tables = beamform(voltages, position, steering, devices, *parts[1], tables)
    send, terms, mask = last_stage(keep, send)
    send, early = send[:, :split], send[:, split:]
    arrived, early = lax.optimization_barrier((arrived, early))
    early_arrived = across(early, mask)
    own, halo = ended(first_terms, arrived, [(i, (i + 1) % steps) for i in range(steps)])
    send, own = lax.optimization_barrier((send, own))
    late_arrived = across(send, mask)
    owns.append(own)
    halos.append(halo)
    own, halo = ended([term[:, split:] for term in terms], early_arrived, [(i, i + 1) for i in range(steps - 1)])
    late = added(*[term[0, :split] for term in terms], late_arrived[0])
    owns.append(jnp.concatenate([late, own], axis=0))
    halos.append(halo)
    own = owns[-1]
    starts = [start for start, _ in parts]
    frames, _, beams, _ = own.shape
    single = jnp.float32
    sums = jax.ShapeDtypeStruct((2, frames, beams, channels), single)
    own_sums = jax.ShapeDtypeStruct((2, frames * beams, channels), single)
    others = small_call(functools.partial(part_kernel, starts[:-1], False), frames * beams, (*owns[:-1], basis), own_sums)
    args = (*owns[-1:], others, basis, synthesis_taps)
    filtered = small_call(functools.partial(own_kernel, starts[-1:]), frames * beams, args, sums)
    part_sums = jax.ShapeDtypeStruct((2, before * beams, channels), single)
    others = small_call(functools.partial(part_kernel, starts[:-1], True), before * beams, (*halos[:-1], basis), part_sums)
    out_shape = jax.ShapeDtypeStruct((2, beams, frames, channels), jnp.bfloat16)
    slabs = channels // 256
    scratch = [
        pltpu.VMEM((slabs, 2, 256 // LANES, frames * beams, LANES), single),
        pltpu.VMEM((slabs, 2, beams, frames, 256), jnp.bfloat16),
        pltpu.SemaphoreType.DMA((slabs,)),
    ]
    args = (*halos[-1:], others, filtered, basis, synthesis_taps)
    return small_call(functools.partial(taps_kernel, starts[-1:]), before * beams, args, out_shape, scratch, pltpu.HBM)


def solution(mesh):
    return jax.shard_map(
        steps_on_device,
        mesh=mesh,
        in_specs=(P(None, ("group", "tm"), "chan", None), P(), P("group", None), P()),
        out_specs=P(None, "chan", ("group", "tm"), None),
        check_vma=False,
    )
```

```python
import functools
import math

import jax
import jax.numpy as jnp
from jax import lax
from jax.experimental import pallas as pl
from jax.experimental.pallas import tpu as pltpu
from jax.sharding import PartitionSpec as P


PHASES = 4096
LANES = 128
HALF = 32
SLAB = 16
TABLE = jnp.float32
BEAM_LIMIT = 24
AHEAD = 2
START_CENTRES = 2


def turn(phase, steps):
    quarter = steps // 4
    shift = quarter.bit_length() - 1
    quadrant = lax.shift_right_logical(phase + quarter // 2, shift)
    rest = (phase - lax.shift_left(quadrant, shift)).astype(jnp.float32) * (2.0 * math.pi / steps)
    square = rest * rest
    sine = rest * (1.0 + square * (-1.6666666e-1 + square * (8.3333310e-3 + square * (-1.9840874e-4 + square * 2.7525562e-6))))
    cosine = 1.0 + square * (-0.5 + square * (4.1666666e-2 + square * (-1.3888889e-3 + square * (2.4801587e-5 - square * 2.7557319e-7))))
    odd = (quadrant & 1) == 1
    real = jnp.where(odd, sine, cosine)
    imag = jnp.where(odd, cosine, sine)
    real = jnp.where(((quadrant + 1) & 2) == 2, -real, real)
    imag = jnp.where((quadrant & 2) == 2, -imag, imag)
    return real, imag


def times(a, b):
    return a[0] * b[0] - a[1] * b[1], a[0] * b[1] + a[1] * b[0]


def table_kernel_part(copy, position_hbm, steering_hbm, position, steering, small_arrivals, offset_tables, centre_tables, stride_table, own_beams):
    feeds, beams = offset_tables.shape[2:]
    here = lax.axis_index("chan")
    position_copy = pltpu.make_async_copy(position_hbm, position, small_arrivals.at[0])
    steering_copy = pltpu.make_async_copy(steering_hbm, steering, small_arrivals.at[1])
    position_copy.start()
    steering_copy.start()
    copy.start()
    position_copy.wait()
    steering_copy.wait()

    def column(axis):
        start = here * feeds if position.shape[1] > feeds else 0
        row = position[axis : axis + 1, pl.ds(pl.multiple_of(start, LANES), feeds)].astype(jnp.float32)
        return jnp.transpose(jnp.broadcast_to(row, (beams, feeds))).astype(jnp.int32)

    lane = lax.broadcasted_iota(jnp.int32, steering.shape, 1)
    aim = steering[...]
    size = own_beams
    while size < beams:
        upper = (lane & size) != 0
        swapped = jnp.where(upper, pltpu.roll(aim, size, 1), pltpu.roll(aim, beams - size, 1))
        aim = jnp.where((here & (size // own_beams)) != 0, swapped, aim)
        size *= 2
    total = column(0) * aim[0:1, :] + column(1) * aim[1:2, :]
    offset_tables[0, 0] = (total & (PHASES - 1)).astype(TABLE)

    def one_slab(index, carry):
        at = pl.multiple_of(index * SLAB, SLAB)
        delay = offset_tables[0, 0, pl.ds(at, SLAB), :].astype(jnp.int32)
        half_step = turn(delay, 2 * PHASES)
        state = half_step
        advance = times(half_step, half_step)
        for offset in range(HALF):
            offset_tables[0, offset, pl.ds(at, SLAB), :] = state[0].astype(TABLE)
            offset_tables[1, offset, pl.ds(at, SLAB), :] = state[1].astype(TABLE)
            if offset + 1 < HALF:
                state = times(state, advance)
        state = turn(((2 * HALF - 1) * delay) & (2 * PHASES - 1), 2 * PHASES)
        advance = turn((4 * HALF * delay) & (2 * PHASES - 1), 2 * PHASES)
        stride_table[0, pl.ds(at, SLAB), :] = advance[0]
        stride_table[1, pl.ds(at, SLAB), :] = advance[1]
        for centre in range(START_CENTRES):
            centre_tables[0, centre, pl.ds(at, SLAB), :] = state[0].astype(TABLE)
            centre_tables[1, centre, pl.ds(at, SLAB), :] = state[1].astype(TABLE)
            if centre + 1 < START_CENTRES:
                state = times(state, advance)
        return carry

    lax.fori_loop(0, feeds // SLAB, one_slab, 0)


def beam_kernel(first, make_tables, *refs):
    if make_tables:
        position_hbm, steering_hbm, voltages, keep, send, offset_tables, centre_tables, staged = refs[:8]
        position, steering, small_arrivals, arrivals, stride_table = refs[8:13]
    else:
        offset_tables, centre_tables, staged, keep, send = refs[:5]
    both_rows, both_sums = refs[-2:]
    feeds, beams = offset_tables.shape[2:]
    frames = staged.shape[1]
    stride = 2 * frames
    block = LANES
    devices = 2 * keep.shape[0]
    own_beams = beams // devices
    before = first // block
    blocks = keep.shape[4] // block

    if make_tables:
        copy = pltpu.make_async_copy(voltages, staged, arrivals.at[0])
        table_kernel_part(copy, position_hbm, steering_hbm, position, steering, small_arrivals, offset_tables, centre_tables, stride_table, own_beams)
        copy.wait()

    width = min(feeds, LANES)
    scale = 1.0 / math.sqrt(feeds * devices)
    sign = jnp.where(lax.broadcasted_iota(jnp.int32, (stride, beams), 0) < frames, -1.0, 1.0)

    def take(index, rows, slot):
        for at in range(feeds // width):
            lanes = pl.ds(pl.multiple_of((before + index) * block, block), block)
            piece = staged[slot // frames, slot % frames, at * width : (at + 1) * width, lanes].astype(jnp.float32)
            if width < LANES:
                piece = jnp.concatenate([piece, jnp.zeros((LANES - width, block), jnp.float32)], axis=0)
            rows[at, pl.ds(slot, block, stride=stride), :] = jnp.transpose(piece)

    def give(index, sums, slot):
        piece = jnp.transpose(sums[pl.ds(slot, block, stride=stride), :] * scale)
        for relative in range(devices):
            value = piece[relative * own_beams : (relative + 1) * own_beams, :].astype(jnp.bfloat16)
            out = send if relative % 2 else keep
            out[relative // 2, slot % frames, slot // frames, :, pl.ds(pl.multiple_of(index * block, block), block)] = value

    def quarter_turn(value):
        return pltpu.roll(value, frames, 0) * sign

    def dot(a, b):
        return jnp.dot(a, b, preferred_element_type=jnp.float32)

    def lhs(rows, local, offset):
        upper = local * 2 * HALF + HALF + offset
        lower = local * 2 * HALF + HALF - 1 - offset
        pieces = []
        for at in range(feeds // width):
            top = rows[at, upper * stride : (upper + 1) * stride, :]
            bottom = rows[at, lower * stride : (lower + 1) * stride, :]
            pieces.append(jnp.concatenate([top, bottom], axis=0))
        return jnp.concatenate(pieces, axis=1).astype(jnp.bfloat16)[:, :feeds]

    def pair(left, sums, cosine, sine, local, offset):
        upper = local * 2 * HALF + HALF + offset
        lower = local * 2 * HALF + HALF - 1 - offset
        small_cosine = offset_tables[0, offset].astype(jnp.bfloat16)
        small_sine = offset_tables[1, offset].astype(jnp.bfloat16)
        straight = dot(left, jnp.concatenate([cosine * small_cosine, sine * small_sine], axis=1))
        crossed = dot(left, jnp.concatenate([sine * small_cosine, cosine * small_sine], axis=1))
        a, b, c, d = straight[:, :beams], straight[:, beams:], crossed[:, :beams], crossed[:, beams:]
        more = quarter_turn(c[:stride] + d[:stride])
        less = quarter_turn(c[stride:] - d[stride:])
        sums[upper * stride : (upper + 1) * stride, :] = a[:stride] - b[:stride] + more
        sums[lower * stride : (lower + 1) * stride, :] = a[stride:] + b[stride:] + less

    growth = -(-(centre_tables.shape[1] - START_CENTRES) // blocks)

    def grow(index, at):
        slab = slice(at * SLAB, (at + 1) * SLAB)
        advance = (stride_table[0, slab, :], stride_table[1, slab, :])
        start = START_CENTRES - 1 + index * growth
        state = (centre_tables[0, start, slab, :], centre_tables[1, start, slab, :])
        for more in range(growth):
            state = times(state, advance)
            target = start + 1 + more
            centre_tables[0, target, slab, :] = state[0]
            centre_tables[1, target, slab, :] = state[1]

    def one_block(index, parity):
        rows, sums = both_rows.at[parity], both_sums.at[parity]
        other_rows, other_sums = both_rows.at[1 - parity], both_sums.at[1 - parity]
        locals_ = block // (2 * HALF)
        every = HALF * locals_ // stride
        lefts = [(local, offset) for local in range(locals_) for offset in range(HALF)]
        ready = [lhs(rows, *at) for at in lefts[:AHEAD]]
        for count, (local, offset) in enumerate(lefts):
            if offset == 0:
                centre = (before + index) * locals_ + local
                cosine = centre_tables[0, centre].astype(jnp.bfloat16)
                sine = centre_tables[1, centre].astype(jnp.bfloat16)
            if count % every == 0:
                give(jnp.maximum(index - 1, 0), other_sums, count // every)
                take(jnp.minimum(index + 1, blocks - 1), other_rows, count // every)
            if make_tables and count % 2 == 1 and count // 2 < feeds // SLAB:
                grow(index, count // 2)
            if count + AHEAD < len(lefts):
                ready.append(lhs(rows, *lefts[count + AHEAD]))
            pair(ready[count], sums, cosine, sine, local, offset)

    for slot in range(stride):
        take(0, both_rows.at[0], slot)

    def two_blocks(index, carry):
        one_block(2 * index, 0)
        one_block(2 * index + 1, 1)
        return carry

    lax.fori_loop(0, blocks // 2, two_blocks, 0)
    if blocks % 2:
        one_block(blocks - 1, 0)
    for slot in range(stride):
        give(blocks - 1, both_sums.at[(blocks - 1) & 1], slot)


def beamform(voltages, position, steering, devices, first, count, tables):
    _, frames, feeds, channels = voltages.shape
    beams = steering.shape[1]
    width = min(feeds, LANES)
    shape = jax.ShapeDtypeStruct((devices // 2, frames, 2, beams // devices, count), jnp.bfloat16)
    rows = pltpu.VMEM((2, feeds // width, LANES * 2 * frames, LANES), jnp.float32)
    sums = pltpu.VMEM((2, LANES * 2 * frames, beams), jnp.float32)
    work = 2 * frames * 2 * feeds * beams * count
    whole = pl.BlockSpec(memory_space=pltpu.VMEM)
    anywhere = pl.BlockSpec(memory_space=pltpu.HBM)
    out_shape = [shape, shape]
    growth = -(-(channels // (2 * HALF) - START_CENTRES) // (count // LANES))
    scratch = []
    if tables is None:
        out_shape += [
            jax.ShapeDtypeStruct((2, HALF, feeds, beams), TABLE),
            jax.ShapeDtypeStruct((2, START_CENTRES + growth * (count // LANES), feeds, beams), TABLE),
            jax.ShapeDtypeStruct(voltages.shape, jnp.bfloat16),
        ]
        scratch += [
            pltpu.VMEM(position.shape, jnp.int32),
            pltpu.VMEM(steering.shape, jnp.int32),
            pltpu.SemaphoreType.DMA((2,)),
            pltpu.SemaphoreType.DMA((1,)),
            pltpu.VMEM((2, feeds, beams), jnp.float32),
        ]
        position = pltpu.with_memory_space_constraint(position, pltpu.HBM)
        steering = pltpu.with_memory_space_constraint(steering, pltpu.HBM)
        args, in_specs = (position, steering, voltages), [anywhere] * 3
    else:
        args, in_specs = tables, [whole] * 3
    out = pl.pallas_call(
        functools.partial(beam_kernel, first, tables is None),
        in_specs=in_specs,
        out_specs=[whole] * len(out_shape),
        out_shape=out_shape,
        scratch_shapes=scratch
        + [rows, sums],
        compiler_params=pltpu.CompilerParams(vmem_limit_bytes=BEAM_LIMIT * 2**20),
        cost_estimate=pl.CostEstimate(flops=32 * work, bytes_accessed=4 * 2 * frames * feeds * count, transcendentals=0),
        name="beam",
    )(*args)
    return out[0], out[1], out[2:] if tables is None else tables


def basis_kernel(basis, small):
    channels = basis.shape[0]
    width = small.shape[3]
    group = small.shape[2]

    for first in range(0, channels, width):

        def phases(rows, factor):
            row = lax.broadcasted_iota(jnp.int32, (rows, width), 0) * factor
            column = first + lax.broadcasted_iota(jnp.int32, (rows, width), 1)
            return (row * column) & (channels - 1)

        slab = first // width
        small[slab, 0], small[slab, 1] = turn(phases(group, 1), channels)
        count = channels // group
        large = turn(phases(count, group), channels)
        for at in range(count):
            real, imag = times((large[0][at : at + 1], large[1][at : at + 1]), (small[slab, 0], small[slab, 1]))
            basis[at * group : (at + 1) * group, pl.ds(first, width)] = real.astype(jnp.bfloat16)
            basis[at * group : (at + 1) * group, pl.ds(channels + first, width)] = imag.astype(jnp.bfloat16)


def make_basis(channels):
    return pl.pallas_call(
        basis_kernel,
        out_specs=pl.BlockSpec(memory_space=pltpu.VMEM),
        out_shape=jax.ShapeDtypeStruct((channels, 2 * channels), jnp.bfloat16),
        scratch_shapes=[pltpu.VMEM((channels // 256, 2, 32, 256), jnp.float32)],
        compiler_params=pltpu.CompilerParams(vmem_limit_bytes=8 * 2**20),
        cost_estimate=pl.CostEstimate(flops=2**30, bytes_accessed=4 * channels * channels, transcendentals=0),
        name="basis",
    )()


def transform(pieces, starts, basis, first, width):
    frames, _, beams, _ = pieces[0].shape
    channels = basis.shape[0]
    total = None
    for piece, start in zip(pieces, starts):
        count = piece.shape[3]
        rows = jnp.concatenate([piece[t, part] for part in range(2) for t in range(frames)], axis=0)
        for part in range(2):
            column = part * channels + first
            columns = pl.ds(column if isinstance(column, int) else pl.multiple_of(column, width), width)
            product = jnp.dot(rows, basis[start : start + count, columns], preferred_element_type=jnp.float32)
            total = [None, None] if total is None else total
            total[part] = product if total[part] is None else total[part] + product
    half = frames * beams
    return total[0][:half] - total[1][half:], total[1][:half] + total[0][half:]


def own_kernel(starts, *refs):
    pieces, others, basis, taps, out = refs[:-4], refs[-4], refs[-3], refs[-2], refs[-1]
    frames, _, beams, _ = pieces[0].shape
    channels = basis.shape[0]
    width = min(256, channels)
    scale = 1.0 / math.sqrt(channels)

    for first in range(0, channels, width):
        for part, value in enumerate(transform(pieces, starts, basis, first, width)):
            value = ((value + others[part, :, pl.ds(first, width)]) * scale).astype(jnp.bfloat16).astype(jnp.float32)
            for t in range(frames):
                total = None
                for k in range(min(t + 1, taps.shape[0])):
                    term = taps[k : k + 1, pl.ds(first, width)] * value[(t - k) * beams : (t - k + 1) * beams]
                    total = term if total is None else total + term
                out[part, t, :, pl.ds(first, width)] = total


def part_kernel(starts, wraps, *refs):
    pieces, basis, out = refs[:-2], refs[-2], refs[-1]
    channels = basis.shape[0]
    width = min(256, channels)

    def one_slab(index, carry):
        first = pl.multiple_of(index * width, width)
        for part, value in enumerate(transform(pieces, starts, basis, first, width)):
            out[part, :, pl.ds(first, width)] = jnp.where(lax.axis_index("tm") == 0, 0.0, value) if wraps else value
        return carry

    lax.fori_loop(0, channels // width, one_slab, 0)


def taps_kernel(starts, *refs):
    pieces, others, own, basis, taps, out = refs[:-8], refs[-8], refs[-7], refs[-6], refs[-5], refs[-4]
    turned, result, departures = refs[-3:]
    before, _, beams, _ = pieces[0].shape
    channels = basis.shape[0]
    frames = own.shape[1]
    width = min(256, channels)
    size = beams // departures.shape[1]
    scale = 1.0 / math.sqrt(channels)

    def departure(part, at):
        place = pl.ds(at * size, size)
        return pltpu.make_async_copy(result.at[part, place], out.at[part, place], departures.at[part, at])

    values = []
    for first in range(0, channels, width):
        both = transform(pieces, starts, basis, first, width)
        lanes = pl.ds(first, width)
        values.append([((both[part] + others[part, :, lanes]) * scale).astype(jnp.bfloat16).astype(jnp.float32) for part in range(2)])
    for part in range(2):
        for group in range(beams // size):
            for index, first in enumerate(range(0, channels, width)):
                lanes = pl.ds(first, width)
                for t in range(frames):
                    total = own[part, t, group * size : (group + 1) * size, lanes]
                    for k in range(t + 1, taps.shape[0]):
                        at = (before + t - k) * beams + group * size
                        total = total + taps[k : k + 1, lanes] * values[index][part][at : at + size]
                    for at in range(width // LANES):
                        piece = total[:, at * LANES : (at + 1) * LANES]
                        turned[part, group, first // LANES + at, pl.ds(t, size, stride=frames), :] = piece
                for at in range(first // LANES, (first + width) // LANES):
                    value = turned[part, group, at].reshape(size, frames, LANES).astype(jnp.bfloat16)
                    result[part, group * size : (group + 1) * size, :, at * LANES : (at + 1) * LANES] = value
            departure(part, group).start()
    for part in range(2):
        for group in range(beams // size):
            departure(part, group).wait()


def small_call(kernel, rows, args, out_shape, scratch=(), space=pltpu.VMEM):
    channels = out_shape.shape[-1]
    whole = pl.BlockSpec(memory_space=pltpu.VMEM)
    return pl.pallas_call(
        kernel,
        in_specs=[whole] * len(args),
        out_specs=pl.BlockSpec(memory_space=space),
        out_shape=out_shape,
        scratch_shapes=scratch,
        compiler_params=pltpu.CompilerParams(vmem_limit_bytes=12 * 2**20),
        cost_estimate=pl.CostEstimate(flops=8 * rows * channels**2, bytes_accessed=4 * channels**2, transcendentals=0),
    )(*args)


def added(*terms):
    return sum(term.astype(jnp.float32) for term in terms).astype(jnp.bfloat16)


def steps_on_device(voltages, feed_position, beam_steering, synthesis_taps):
    devices = lax.axis_size("chan")
    steps = lax.axis_size("tm")
    taps = synthesis_taps.shape[0]
    before = taps - 1
    feeds = voltages.shape[2]
    position = feed_position.T
    if feeds % LANES:
        position = lax.dynamic_slice_in_dim(position, lax.axis_index("chan") * feeds, feeds, 1)
    channels = voltages.shape[3]
    later = max(1, 3 * channels // (8 * LANES)) * LANES
    parts = [(0, channels - later), (channels - later, later)]
    basis = make_basis(channels)
    steering = beam_steering.T
    owns = []
    halos = []

    def across(value, mask):
        return lax.ppermute(value, "chan", [(i, i ^ mask) for i in range(devices)])

    def last_stage(keep, send):
        terms = [keep]
        mask = 1
        while 2 * mask < devices:
            terms.append(across(send, mask))
            send = added(*[term[1::2] for term in terms])
            terms = [term[0::2] for term in terms]
            mask *= 2
        return send, terms, mask

    def ended(terms, arrived, hops):
        own = lax.optimization_barrier(added(*[term[0] for term in terms], arrived[0]))
        return own, lax.ppermute(own[own.shape[0] - before :], "tm", hops)

    voltages = pltpu.with_memory_space_constraint(voltages, pltpu.HBM)
    split = voltages.shape[1] - before
    keep, send, tables = beamform(voltages, position, steering, devices, *parts[0], None)
    send, first_terms, mask = last_stage(keep, send)
    tables, send = lax.optimization_barrier((tables, send))
    arrived = across(send, mask)
    keep, send, tables = beamform(voltages, position, steering, devices, *parts[1], tables)
    send, terms, mask = last_stage(keep, send)
    send, early = send[:, :split], send[:, split:]
    arrived, early = lax.optimization_barrier((arrived, early))
    early_arrived = across(early, mask)
    own, halo = ended(first_terms, arrived, [(i, (i + 1) % steps) for i in range(steps)])
    send, own = lax.optimization_barrier((send, own))
    late_arrived = across(send, mask)
    owns.append(own)
    halos.append(halo)
    own, halo = ended([term[:, split:] for term in terms], early_arrived, [(i, i + 1) for i in range(steps - 1)])
    late = added(*[term[0, :split] for term in terms], late_arrived[0])
    owns.append(jnp.concatenate([late, own], axis=0))
    halos.append(halo)
    own = owns[-1]
    starts = [start for start, _ in parts]
    frames, _, beams, _ = own.shape
    single = jnp.float32
    sums = jax.ShapeDtypeStruct((2, frames, beams, channels), single)
    own_sums = jax.ShapeDtypeStruct((2, frames * beams, channels), single)
    others = small_call(functools.partial(part_kernel, starts[:-1], False), frames * beams, (*owns[:-1], basis), own_sums)
    args = (*owns[-1:], others, basis, synthesis_taps)
    filtered = small_call(functools.partial(own_kernel, starts[-1:]), frames * beams, args, sums)
    part_sums = jax.ShapeDtypeStruct((2, before * beams, channels), single)
    others = small_call(functools.partial(part_kernel, starts[:-1], True), before * beams, (*halos[:-1], basis), part_sums)
    out_shape = jax.ShapeDtypeStruct((2, beams, frames, channels), jnp.bfloat16)
    groups = 2 if beams % 16 == 0 else 1
    scratch = [
        pltpu.VMEM((2, groups, channels // LANES, frames * beams // groups, LANES), single),
        pltpu.VMEM((2, beams, frames, channels), jnp.bfloat16),
        pltpu.SemaphoreType.DMA((2, groups)),
    ]
    args = (*halos[-1:], others, filtered, basis, synthesis_taps)
    return small_call(functools.partial(taps_kernel, starts[-1:]), before * beams, args, out_shape, scratch, pltpu.HBM)


def solution(mesh):
    return jax.shard_map(
        steps_on_device,
        mesh=mesh,
        in_specs=(P(None, ("group", "tm"), "chan", None), P(), P("group", None), P()),
        out_specs=P(None, "chan", ("group", "tm"), None),
        check_vma=False,
    )
```

```python
import functools
import math

import jax
import jax.numpy as jnp
from jax import lax
from jax.experimental import pallas as pl
from jax.experimental.pallas import tpu as pltpu
from jax.sharding import PartitionSpec as P


PHASES = 4096
LANES = 128
HALF = 32
SLAB = 16
TABLE = jnp.float32
BEAM_LIMIT = 24
AHEAD = 2


def turn(phase, steps):
    quarter = steps // 4
    shift = quarter.bit_length() - 1
    quadrant = lax.shift_right_logical(phase + quarter // 2, shift)
    rest = (phase - lax.shift_left(quadrant, shift)).astype(jnp.float32) * (2.0 * math.pi / steps)
    square = rest * rest
    sine = rest * (1.0 + square * (-1.6666666e-1 + square * (8.3333310e-3 + square * (-1.9840874e-4 + square * 2.7525562e-6))))
    cosine = 1.0 + square * (-0.5 + square * (4.1666666e-2 + square * (-1.3888889e-3 + square * (2.4801587e-5 - square * 2.7557319e-7))))
    odd = (quadrant & 1) == 1
    real = jnp.where(odd, sine, cosine)
    imag = jnp.where(odd, cosine, sine)
    real = jnp.where(((quadrant + 1) & 2) == 2, -real, real)
    imag = jnp.where((quadrant & 2) == 2, -imag, imag)
    return real, imag


def times(a, b):
    return a[0] * b[0] - a[1] * b[1], a[0] * b[1] + a[1] * b[0]


def table_kernel_part(copy, position_hbm, steering_hbm, position, steering, small_arrivals, offset_tables, centre_tables, own_beams):
    feeds, beams = offset_tables.shape[2:]
    centres = centre_tables.shape[1]
    here = lax.axis_index("chan")
    position_copy = pltpu.make_async_copy(position_hbm, position, small_arrivals.at[0])
    steering_copy = pltpu.make_async_copy(steering_hbm, steering, small_arrivals.at[1])
    position_copy.start()
    steering_copy.start()
    copy.start()
    position_copy.wait()
    steering_copy.wait()

    def column(axis):
        start = here * feeds if position.shape[1] > feeds else 0
        row = position[axis : axis + 1, pl.ds(pl.multiple_of(start, LANES), feeds)].astype(jnp.float32)
        return jnp.transpose(jnp.broadcast_to(row, (beams, feeds))).astype(jnp.int32)

    lane = lax.broadcasted_iota(jnp.int32, steering.shape, 1)
    aim = steering[...]
    size = own_beams
    while size < beams:
        upper = (lane & size) != 0
        swapped = jnp.where(upper, pltpu.roll(aim, size, 1), pltpu.roll(aim, beams - size, 1))
        aim = jnp.where((here & (size // own_beams)) != 0, swapped, aim)
        size *= 2
    total = column(0) * aim[0:1, :] + column(1) * aim[1:2, :]
    offset_tables[0, 0] = (total & (PHASES - 1)).astype(TABLE)

    def one_slab(index, carry):
        at = pl.multiple_of(index * SLAB, SLAB)
        delay = offset_tables[0, 0, pl.ds(at, SLAB), :].astype(jnp.int32)
        half_step = turn(delay, 2 * PHASES)
        state = half_step
        advance = times(half_step, half_step)
        for offset in range(HALF):
            offset_tables[0, offset, pl.ds(at, SLAB), :] = state[0].astype(TABLE)
            offset_tables[1, offset, pl.ds(at, SLAB), :] = state[1].astype(TABLE)
            if offset + 1 < HALF:
                state = times(state, advance)
        state = turn(((2 * HALF - 1) * delay) & (2 * PHASES - 1), 2 * PHASES)
        advance = turn((4 * HALF * delay) & (2 * PHASES - 1), 2 * PHASES)
        for centre in range(centres):
            centre_tables[0, centre, pl.ds(at, SLAB), :] = state[0].astype(TABLE)
            centre_tables[1, centre, pl.ds(at, SLAB), :] = state[1].astype(TABLE)
            if centre + 1 < centres:
                state = times(state, advance)
        return carry

    lax.fori_loop(0, feeds // SLAB, one_slab, 0)


def beam_kernel(first, make_tables, *refs):
    if make_tables:
        position_hbm, steering_hbm, voltages, keep, send, offset_tables, centre_tables, staged = refs[:8]
        position, steering, small_arrivals, arrivals = refs[8:12]
    else:
        offset_tables, centre_tables, staged, keep, send = refs[:5]
    both_rows, both_sums = refs[-2:]
    feeds, beams = offset_tables.shape[2:]
    frames = staged.shape[1]
    stride = 2 * frames
    block = LANES
    devices = 2 * keep.shape[0]
    own_beams = beams // devices
    before = first // block
    blocks = keep.shape[4] // block

    if make_tables:
        copy = pltpu.make_async_copy(voltages, staged, arrivals.at[0])
        table_kernel_part(copy, position_hbm, steering_hbm, position, steering, small_arrivals, offset_tables, centre_tables, own_beams)
        copy.wait()

    width = min(feeds, LANES)
    scale = 1.0 / math.sqrt(feeds * devices)
    sign = jnp.where(lax.broadcasted_iota(jnp.int32, (stride, beams), 0) < frames, -1.0, 1.0)

    def take(index, rows, slot):
        for at in range(feeds // width):
            lanes = pl.ds(pl.multiple_of((before + index) * block, block), block)
            piece = staged[slot // frames, slot % frames, at * width : (at + 1) * width, lanes].astype(jnp.float32)
            if width < LANES:
                piece = jnp.concatenate([piece, jnp.zeros((LANES - width, block), jnp.float32)], axis=0)
            rows[at, pl.ds(slot, block, stride=stride), :] = jnp.transpose(piece)

    def give(index, sums, slot):
        piece = jnp.transpose(sums[pl.ds(slot, block, stride=stride), :] * scale)
        for relative in range(devices):
            value = piece[relative * own_beams : (relative + 1) * own_beams, :].astype(jnp.bfloat16)
            out = send if relative % 2 else keep
            out[relative // 2, slot % frames, slot // frames, :, pl.ds(pl.multiple_of(index * block, block), block)] = value

    def quarter_turn(value):
        return pltpu.roll(value, frames, 0) * sign

    def dot(a, b):
        return jnp.dot(a, b, preferred_element_type=jnp.float32)

    def lhs(rows, local, offset):
        upper = local * 2 * HALF + HALF + offset
        lower = local * 2 * HALF + HALF - 1 - offset
        pieces = []
        for at in range(feeds // width):
            top = rows[at, upper * stride : (upper + 1) * stride, :]
            bottom = rows[at, lower * stride : (lower + 1) * stride, :]
            pieces.append(jnp.concatenate([top, bottom], axis=0))
        return jnp.concatenate(pieces, axis=1).astype(jnp.bfloat16)[:, :feeds]

    def pair(left, sums, cosine, sine, local, offset):
        upper = local * 2 * HALF + HALF + offset
        lower = local * 2 * HALF + HALF - 1 - offset
        small_cosine = offset_tables[0, offset].astype(jnp.bfloat16)
        small_sine = offset_tables[1, offset].astype(jnp.bfloat16)
        straight = dot(left, jnp.concatenate([cosine * small_cosine, sine * small_sine], axis=1))
        crossed = dot(left, jnp.concatenate([sine * small_cosine, cosine * small_sine], axis=1))
        a, b, c, d = straight[:, :beams], straight[:, beams:], crossed[:, :beams], crossed[:, beams:]
        more = quarter_turn(c[:stride] + d[:stride])
        less = quarter_turn(c[stride:] - d[stride:])
        sums[upper * stride : (upper + 1) * stride, :] = a[:stride] - b[:stride] + more
        sums[lower * stride : (lower + 1) * stride, :] = a[stride:] + b[stride:] + less

    def one_block(index, parity):
        rows, sums = both_rows.at[parity], both_sums.at[parity]
        other_rows, other_sums = both_rows.at[1 - parity], both_sums.at[1 - parity]
        locals_ = block // (2 * HALF)
        every = HALF * locals_ // stride
        lefts = [(local, offset) for local in range(locals_) for offset in range(HALF)]
        ready = [lhs(rows, *at) for at in lefts[:AHEAD]]
        for count, (local, offset) in enumerate(lefts):
            if offset == 0:
                centre = (before + index) * locals_ + local
                cosine = centre_tables[0, centre].astype(jnp.bfloat16)
                sine = centre_tables[1, centre].astype(jnp.bfloat16)
            if count % every == 0:
                give(jnp.maximum(index - 1, 0), other_sums, count // every)
                take(jnp.minimum(index + 1, blocks - 1), other_rows, count // every)
            if count + AHEAD < len(lefts):
                ready.append(lhs(rows, *lefts[count + AHEAD]))
            pair(ready[count], sums, cosine, sine, local, offset)

    for slot in range(stride):
        take(0, both_rows.at[0], slot)

    def two_blocks(index, carry):
        one_block(2 * index, 0)
        one_block(2 * index + 1, 1)
        return carry

    lax.fori_loop(0, blocks // 2, two_blocks, 0)
    if blocks % 2:
        one_block(blocks - 1, 0)
    for slot in range(stride):
        give(blocks - 1, both_sums.at[(blocks - 1) & 1], slot)


def beamform(voltages, position, steering, devices, first, count, tables):
    _, frames, feeds, channels = voltages.shape
    beams = steering.shape[1]
    width = min(feeds, LANES)
    shape = jax.ShapeDtypeStruct((devices // 2, frames, 2, beams // devices, count), jnp.bfloat16)
    rows = pltpu.VMEM((2, feeds // width, LANES * 2 * frames, LANES), jnp.float32)
    sums = pltpu.VMEM((2, LANES * 2 * frames, beams), jnp.float32)
    work = 2 * frames * 2 * feeds * beams * count
    whole = pl.BlockSpec(memory_space=pltpu.VMEM)
    anywhere = pl.BlockSpec(memory_space=pltpu.HBM)
    out_shape = [shape, shape]
    scratch = []
    if tables is None:
        out_shape += [
            jax.ShapeDtypeStruct((2, HALF, feeds, beams), TABLE),
            jax.ShapeDtypeStruct((2, channels // (2 * HALF), feeds, beams), TABLE),
            jax.ShapeDtypeStruct(voltages.shape, jnp.bfloat16),
        ]
        scratch += [
            pltpu.VMEM(position.shape, jnp.int32),
            pltpu.VMEM(steering.shape, jnp.int32),
            pltpu.SemaphoreType.DMA((2,)),
            pltpu.SemaphoreType.DMA((1,)),
        ]
        position = pltpu.with_memory_space_constraint(position, pltpu.HBM)
        steering = pltpu.with_memory_space_constraint(steering, pltpu.HBM)
        args, in_specs = (position, steering, voltages), [anywhere] * 3
    else:
        args, in_specs = tables, [whole] * 3
    out = pl.pallas_call(
        functools.partial(beam_kernel, first, tables is None),
        in_specs=in_specs,
        out_specs=[whole] * len(out_shape),
        out_shape=out_shape,
        scratch_shapes=scratch
        + [rows, sums],
        compiler_params=pltpu.CompilerParams(vmem_limit_bytes=BEAM_LIMIT * 2**20),
        cost_estimate=pl.CostEstimate(flops=32 * work, bytes_accessed=4 * 2 * frames * feeds * count, transcendentals=0),
        name="beam",
    )(*args)
    return out[0], out[1], out[2:] if tables is None else tables


def basis_kernel(basis, small):
    channels = basis.shape[0]
    width = small.shape[3]
    group = small.shape[2]

    for first in range(0, channels, width):

        def phases(rows, factor):
            row = lax.broadcasted_iota(jnp.int32, (rows, width), 0) * factor
            column = first + lax.broadcasted_iota(jnp.int32, (rows, width), 1)
            return (row * column) & (channels - 1)

        slab = first // width
        small[slab, 0], small[slab, 1] = turn(phases(group, 1), channels)
        count = channels // group
        large = turn(phases(count, group), channels)
        for at in range(count):
            real, imag = times((large[0][at : at + 1], large[1][at : at + 1]), (small[slab, 0], small[slab, 1]))
            basis[at * group : (at + 1) * group, pl.ds(first, width)] = real.astype(jnp.bfloat16)
            basis[at * group : (at + 1) * group, pl.ds(channels + first, width)] = imag.astype(jnp.bfloat16)


def make_basis(channels):
    return pl.pallas_call(
        basis_kernel,
        out_specs=pl.BlockSpec(memory_space=pltpu.VMEM),
        out_shape=jax.ShapeDtypeStruct((channels, 2 * channels), jnp.bfloat16),
        scratch_shapes=[pltpu.VMEM((channels // 256, 2, 32, 256), jnp.float32)],
        compiler_params=pltpu.CompilerParams(vmem_limit_bytes=8 * 2**20),
        cost_estimate=pl.CostEstimate(flops=2**30, bytes_accessed=4 * channels * channels, transcendentals=0),
        name="basis",
    )()


def transform(pieces, starts, basis, first, width):
    frames, _, beams, _ = pieces[0].shape
    channels = basis.shape[0]
    total = None
    for piece, start in zip(pieces, starts):
        count = piece.shape[3]
        rows = jnp.concatenate([piece[t, part] for part in range(2) for t in range(frames)], axis=0)
        for part in range(2):
            column = part * channels + first
            columns = pl.ds(column if isinstance(column, int) else pl.multiple_of(column, width), width)
            product = jnp.dot(rows, basis[start : start + count, columns], preferred_element_type=jnp.float32)
            total = [None, None] if total is None else total
            total[part] = product if total[part] is None else total[part] + product
    half = frames * beams
    return total[0][:half] - total[1][half:], total[1][:half] + total[0][half:]


def own_kernel(starts, *refs):
    pieces, others, basis, taps, out = refs[:-4], refs[-4], refs[-3], refs[-2], refs[-1]
    frames, _, beams, _ = pieces[0].shape
    channels = basis.shape[0]
    width = min(256, channels)
    scale = 1.0 / math.sqrt(channels)

    for first in range(0, channels, width):
        for part, value in enumerate(transform(pieces, starts, basis, first, width)):
            value = ((value + others[part, :, pl.ds(first, width)]) * scale).astype(jnp.bfloat16).astype(jnp.float32)
            for t in range(frames):
                total = None
                for k in range(min(t + 1, taps.shape[0])):
                    term = taps[k : k + 1, pl.ds(first, width)] * value[(t - k) * beams : (t - k + 1) * beams]
                    total = term if total is None else total + term
                out[part, t, :, pl.ds(first, width)] = total


def part_kernel(starts, wraps, *refs):
    pieces, basis, out = refs[:-2], refs[-2], refs[-1]
    channels = basis.shape[0]
    width = min(256, channels)

    def one_slab(index, carry):
        first = pl.multiple_of(index * width, width)
        for part, value in enumerate(transform(pieces, starts, basis, first, width)):
            out[part, :, pl.ds(first, width)] = jnp.where(lax.axis_index("tm") == 0, 0.0, value) if wraps else value
        return carry

    lax.fori_loop(0, channels // width, one_slab, 0)


def taps_kernel(starts, *refs):
    pieces, others, own, basis, taps, out = refs[:-8], refs[-8], refs[-7], refs[-6], refs[-5], refs[-4]
    turned, result, departures = refs[-3:]
    before, _, beams, _ = pieces[0].shape
    channels = basis.shape[0]
    frames = own.shape[1]
    slabs = departures.shape[0]
    width = channels // slabs
    scale = 1.0 / math.sqrt(channels)

    def departure(index):
        lanes = pl.ds(index * width, width)
        return pltpu.make_async_copy(result.at[index], out.at[:, :, :, lanes], departures.at[index])

    for index in range(slabs):
        lanes = pl.ds(index * width, width)
        for part, value in enumerate(transform(pieces, starts, basis, index * width, width)):
            value = ((value + others[part, :, lanes]) * scale).astype(jnp.bfloat16).astype(jnp.float32)
            for t in range(frames):
                total = own[part, t, :, lanes]
                for k in range(t + 1, taps.shape[0]):
                    at = before + t - k
                    total = total + taps[k : k + 1, lanes] * value[at * beams : (at + 1) * beams]
                for at in range(width // LANES):
                    turned[index, part, at, pl.ds(t, beams, stride=frames), :] = total[:, at * LANES : (at + 1) * LANES]
            for at in range(width // LANES):
                value = turned[index, part, at].reshape(beams, frames, LANES).astype(jnp.bfloat16)
                result[index, part, :, :, at * LANES : (at + 1) * LANES] = value
        departure(index).start()
    for index in range(slabs):
        departure(index).wait()


def small_call(kernel, rows, args, out_shape, scratch=(), space=pltpu.VMEM):
    channels = out_shape.shape[-1]
    whole = pl.BlockSpec(memory_space=pltpu.VMEM)
    return pl.pallas_call(
        kernel,
        in_specs=[whole] * len(args),
        out_specs=pl.BlockSpec(memory_space=space),
        out_shape=out_shape,
        scratch_shapes=scratch,
        compiler_params=pltpu.CompilerParams(vmem_limit_bytes=12 * 2**20),
        cost_estimate=pl.CostEstimate(flops=8 * rows * channels**2, bytes_accessed=4 * channels**2, transcendentals=0),
    )(*args)


def added(*terms):
    return sum(term.astype(jnp.float32) for term in terms).astype(jnp.bfloat16)


def steps_on_device(voltages, feed_position, beam_steering, synthesis_taps):
    devices = lax.axis_size("chan")
    steps = lax.axis_size("tm")
    taps = synthesis_taps.shape[0]
    before = taps - 1
    feeds = voltages.shape[2]
    position = feed_position.T
    if feeds % LANES:
        position = lax.dynamic_slice_in_dim(position, lax.axis_index("chan") * feeds, feeds, 1)
    channels = voltages.shape[3]
    later = max(1, 3 * channels // (8 * LANES)) * LANES
    parts = [(0, channels - later), (channels - later, later)]
    basis = make_basis(channels)
    steering = beam_steering.T
    owns = []
    halos = []

    def across(value, mask):
        return lax.ppermute(value, "chan", [(i, i ^ mask) for i in range(devices)])

    def last_stage(keep, send):
        terms = [keep]
        mask = 1
        while 2 * mask < devices:
            terms.append(across(send, mask))
            send = added(*[term[1::2] for term in terms])
            terms = [term[0::2] for term in terms]
            mask *= 2
        return send, terms, mask

    def ended(terms, arrived, hops):
        own = lax.optimization_barrier(added(*[term[0] for term in terms], arrived[0]))
        return own, lax.ppermute(own[own.shape[0] - before :], "tm", hops)

    voltages = pltpu.with_memory_space_constraint(voltages, pltpu.HBM)
    split = voltages.shape[1] - before
    keep, send, tables = beamform(voltages, position, steering, devices, *parts[0], None)
    send, first_terms, mask = last_stage(keep, send)
    tables, send = lax.optimization_barrier((tables, send))
    arrived = across(send, mask)
    keep, send, tables = beamform(voltages, position, steering, devices, *parts[1], tables)
    send, terms, mask = last_stage(keep, send)
    send, early = send[:, :split], send[:, split:]
    arrived, early = lax.optimization_barrier((arrived, early))
    early_arrived = across(early, mask)
    own, halo = ended(first_terms, arrived, [(i, (i + 1) % steps) for i in range(steps)])
    send, own = lax.optimization_barrier((send, own))
    late_arrived = across(send, mask)
    owns.append(own)
    halos.append(halo)
    own, halo = ended([term[:, split:] for term in terms], early_arrived, [(i, i + 1) for i in range(steps - 1)])
    late = added(*[term[0, :split] for term in terms], late_arrived[0])
    owns.append(jnp.concatenate([late, own], axis=0))
    halos.append(halo)
    own = owns[-1]
    starts = [start for start, _ in parts]
    frames, _, beams, _ = own.shape
    single = jnp.float32
    sums = jax.ShapeDtypeStruct((2, frames, beams, channels), single)
    own_sums = jax.ShapeDtypeStruct((2, frames * beams, channels), single)
    others = small_call(functools.partial(part_kernel, starts[:-1], False), frames * beams, (*owns[:-1], basis), own_sums)
    args = (*owns[-1:], others, basis, synthesis_taps)
    filtered = small_call(functools.partial(own_kernel, starts[-1:]), frames * beams, args, sums)
    part_sums = jax.ShapeDtypeStruct((2, before * beams, channels), single)
    others = small_call(functools.partial(part_kernel, starts[:-1], True), before * beams, (*halos[:-1], basis), part_sums)
    out_shape = jax.ShapeDtypeStruct((2, beams, frames, channels), jnp.bfloat16)
    slabs = channels // 256
    scratch = [
        pltpu.VMEM((slabs, 2, 256 // LANES, frames * beams, LANES), single),
        pltpu.VMEM((slabs, 2, beams, frames, 256), jnp.bfloat16),
        pltpu.SemaphoreType.DMA((slabs,)),
    ]
    args = (*halos[-1:], others, filtered, basis, synthesis_taps)
    return small_call(functools.partial(taps_kernel, starts[-1:]), before * beams, args, out_shape, scratch, pltpu.HBM)


def solution(mesh):
    return jax.shard_map(
        steps_on_device,
        mesh=mesh,
        in_specs=(P(None, ("group", "tm"), "chan", None), P(), P("group", None), P()),
        out_specs=P(None, "chan", ("group", "tm"), None),
        check_vma=False,
    )
```
